768 devices in a mesh: seq: 32 (over y, x), mp: 24 (over z, core).
Axes of the slice: x: 4, y: 8, z: 12, core: 2. Of those that a mesh axis runs over, the one named last changes fastest.
Arguments:
- hidden: bfloat16 [4096, 4096], P('seq'), may hold values from -21 to 21
- w_query: bfloat16 [4096, 3072], P(None, 'mp'), may hold values from -0.09375 to 0.09375
- w_key: bfloat16 [4096, 768], P(None, 'mp'), may hold values from -0.09375 to 0.09375
- w_value: bfloat16 [4096, 768], P(None, 'mp'), may hold values from -0.09375 to 0.09375
- mix_before: float32 [24, 24], replicated, may hold values from -1.25 to 1.25
- mix_after: float32 [24, 24], replicated, may hold values from -1.25 to 1.25
- doc_lengths: int32 [128], replicated, may hold values from 1 to 157, as said below
- doc_owner: int32 [128], replicated, may hold values from 0 to 31, as said below
- loader_order: int32 [4096], replicated, may hold values from 0 to 4095, as said below
Outputs:
- attended: bfloat16 [5120, 3072], P('seq', 'mp')
The draws below stay inside these ranges and needn't reach their ends.
Inputs may be any that keep to these rules, and one draw needn't show every extreme that they name: `doc_lengths`: the lengths of the documents of the packed batch in order; they sum to 4096. `doc_owner`: each shard holds 4 documents; the documents of one shard hold at most 160 tokens together, and some shard holds exactly 160. `loader_order`: A permutation of the packed positions. The 128 rows of one index of seq hold, for every shard, the floor or the ceiling of that shard's tokens divided by the size of seq; so at most 5 rows for one shard, a bound that is reached.
All inputs are finite; a program needn't handle non-finite values.
Results may differ from the reference program's by a relative error of at most 0.012.
The reference program's roundings to bfloat16 on the way count: a program that leaves them out, or rounds other values in their place, can miss the bound.
Values may be sent and summed in bfloat16 or wider, within the bound.
No kernel may reach another device: no remote copies, remote signals or barrier semaphores. Data moves between devices by JAX's collectives and lax.ppermute only.
A program may use at most 32 MiB of HBM per device.

```python
import jax
import jax.numpy as jnp
from jax import lax

D = 4096
HEAD_DIM = 128
GROUP = 4
TOK_DEV = 128
DOCS_DEV = 4
HEADS = 24
KV_HEADS = 6
CAP = 160
TOKENS = 4096
DOCS = 128
N_SEQ = 32


def make_layout(key):
    base = jax.random.fold_in(key, 7)
    spare = CAP - TOK_DEV
    deltas = jax.random.randint(jax.random.fold_in(base, 1), (N_SEQ // 2,), 0, spare + 1)
    deltas = deltas.at[0].set(spare)
    paired = jnp.stack([TOK_DEV + deltas, TOK_DEV - deltas], axis=1).reshape(N_SEQ)
    loads = paired[jax.random.permutation(jax.random.fold_in(base, 2), N_SEQ)].astype(jnp.int32)
    cut_top = (loads - DOCS_DEV)[:, None].astype(jnp.int32)
    cuts = jax.random.randint(jax.random.fold_in(base, 3), (N_SEQ, DOCS_DEV - 1), 0, cut_top + 1)
    cuts = jnp.sort(cuts.astype(jnp.int32), axis=1)
    edges = jnp.concatenate([jnp.zeros((N_SEQ, 1), jnp.int32), cuts, cut_top], axis=1)
    split = (edges[:, 1:] - edges[:, :-1] + 1).astype(jnp.int32)
    forced = jnp.concatenate([jnp.full((N_SEQ, 1), CAP - DOCS_DEV + 1, jnp.int32), jnp.ones((N_SEQ, DOCS_DEV - 1), jnp.int32)], axis=1)
    full_shard = (loads == CAP)[:, None]
    split = jnp.where(full_shard, forced, split)
    grouped = split.reshape(DOCS).astype(jnp.int32)
    owners = jnp.repeat(jnp.arange(N_SEQ, dtype=jnp.int32), DOCS_DEV)
    shuffle_docs = jax.random.permutation(jax.random.fold_in(base, 4), DOCS)
    lengths = grouped[shuffle_docs].astype(jnp.int32)
    owner = owners[shuffle_docs].astype(jnp.int32)
    doc_ends = jnp.cumsum(lengths).astype(jnp.int32)
    starts = doc_ends - lengths
    doc_index = jnp.arange(DOCS, dtype=jnp.int32)
    same_shard = owner[:, None] == owner[None, :]
    before = doc_index[None, :] < doc_index[:, None]
    shard_start = jnp.sum(jnp.where(same_shard & before, lengths[None, :], 0), axis=1).astype(jnp.int32)
    dest_base = (jnp.cumsum(loads) - loads).astype(jnp.int32)
    positions = jnp.arange(TOKENS, dtype=jnp.int32)
    inside = (positions[:, None] >= starts[None, :]) & (positions[:, None] < doc_ends[None, :])
    offsets = dest_base[owner] + shard_start - starts
    listed = jnp.sum(jnp.where(inside, offsets[None, :], 0), axis=1).astype(jnp.int32) + positions
    source = listed % N_SEQ
    within = listed // N_SEQ
    sub_keys = jax.random.split(jax.random.fold_in(base, 5), N_SEQ)
    shuffles = jax.vmap(lambda key_one: jax.random.permutation(key_one, TOK_DEV))(sub_keys).astype(jnp.int32)
    loader_row = source * TOK_DEV + shuffles[source, within]
    loader = jnp.zeros((TOKENS,), jnp.int32).at[loader_row].set(positions)
    return (lengths, owner, loader)


def draw_doc_lengths(key, part):
    return make_layout(key)[0]


def draw_doc_owner(key, part):
    return make_layout(key)[1]


def draw_loader_order(key, part):
    return make_layout(key)[2]


def draw_hidden(key, part):
    base = jax.random.fold_in(key, 11)
    values = jnp.clip(jax.random.normal(jax.random.fold_in(base, 3), (TOKENS, D), jnp.float32), -6.0, 6.0)
    return values.astype(jnp.bfloat16)


def steps_of(stream_key, shape, cuts, low, high):
    factor_of = 1.0
    for dim, parts in cuts:
        heights = jax.random.uniform(jax.random.fold_in(jax.random.fold_in(stream_key, 6), dim), (parts,), jnp.float32, low / len(cuts), high / len(cuts))
        factor_of = factor_of * jnp.repeat(jnp.exp(heights), shape[dim] // parts).reshape((-1,) + (1,) * (len(shape) - 1 - dim))
    return factor_of


def normal_values(key, shape, spread, limit, shards=(), kind=jnp.bfloat16):
    values = jax.random.normal(key, shape, jnp.float32) * spread
    if len(shards) > 0:
        values = steps_of(key, shape, shards, -0.22, 0.18) * values
    return jnp.clip(values, min=-limit, max=limit).astype(kind)


def setup_inputs(seed: int = 0) -> dict:
    streams_of = jax.random.split(jax.random.key(seed), 10)
    return {
        "hidden": draw_hidden(jax.random.fold_in(streams_of[9], 71), 0),
        "w_query": normal_values(streams_of[1], (D, HEADS * HEAD_DIM), D ** -0.5, 0.09375, ((1, 24),)),
        "w_key": normal_values(streams_of[2], (D, KV_HEADS * HEAD_DIM), D ** -0.5, 0.09375, ((1, 24),)),
        "w_value": normal_values(streams_of[3], (D, KV_HEADS * HEAD_DIM), D ** -0.5, 0.09375, ((1, 24),)),
        "mix_before": normal_values(streams_of[4], (HEADS, HEADS), HEADS ** -0.5, 1.25, (), jnp.float32),
        "mix_after": normal_values(streams_of[5], (HEADS, HEADS), HEADS ** -0.5, 1.25, (), jnp.float32),
        "doc_lengths": draw_doc_lengths(jax.random.fold_in(streams_of[9], 71), 0),
        "doc_owner": draw_doc_owner(jax.random.fold_in(streams_of[9], 71), 0),
        "loader_order": draw_loader_order(jax.random.fold_in(streams_of[9], 71), 0),
    }


THETA = 500000.0


def rotate(values, positions, first_col):
    columns = first_col + jnp.arange(values.shape[1])
    within = columns % HEAD_DIM
    pair_index = (within // 2).astype(jnp.float32)
    inv_freq = THETA ** (-2.0 * pair_index / HEAD_DIM)
    angle = positions[:, None].astype(jnp.float32) * inv_freq[None, :]
    partner = values.reshape(values.shape[0], values.shape[1] // 2, 2)[:, :, ::-1]
    partner = (partner * jnp.array([-1.0, 1.0], jnp.float32)).reshape(values.shape)
    return values * jnp.cos(angle) + partner * jnp.sin(angle)


def layout(doc_lengths, doc_owner):
    doc_ends = jnp.cumsum(doc_lengths).astype(jnp.int32)
    starts = doc_ends - doc_lengths
    doc_index = jnp.arange(doc_lengths.shape[0]).astype(jnp.int32)
    same_shard = doc_owner[:, None] == doc_owner[None, :]
    before = doc_index[None, :] < doc_index[:, None]
    shard_start = jnp.sum(jnp.where(same_shard & before, doc_lengths[None, :], 0), axis=1).astype(jnp.int32)
    return starts, doc_ends, shard_start, doc_index


def reference(hidden, w_query, w_key, w_value, mix_before, mix_after, doc_lengths, doc_owner, loader_order):
    starts, doc_ends, shard_start, doc_index = layout(doc_lengths, doc_owner)
    inside = (loader_order[:, None] >= starts[None, :]) & (loader_order[:, None] < doc_ends[None, :])
    target = jnp.sum(jnp.where(inside, doc_owner[None, :], 0), axis=1).astype(jnp.int32)
    doc_pos = loader_order - jnp.sum(jnp.where(inside, starts[None, :], 0), axis=1).astype(jnp.int32)
    slot_pos = jnp.sum(jnp.where(inside, shard_start[None, :], 0), axis=1).astype(jnp.int32) + doc_pos
    row_doc = jnp.sum(jnp.where(inside, doc_index[None, :], 0), axis=1).astype(jnp.int32)
    query_rows = rotate(jnp.dot(hidden, w_query, preferred_element_type=jnp.float32), doc_pos, 0).astype(jnp.bfloat16)
    key_rows = rotate(jnp.dot(hidden, w_key, preferred_element_type=jnp.float32), doc_pos, 0).astype(jnp.bfloat16)
    value_rows = jnp.dot(hidden, w_value, preferred_element_type=jnp.float32).astype(jnp.bfloat16)
    where_to = (target * CAP + slot_pos).astype(jnp.int32)
    slots_all = N_SEQ * CAP
    query_slots = jnp.zeros((slots_all, query_rows.shape[1]), jnp.bfloat16).at[where_to].set(query_rows)
    key_slots = jnp.zeros((slots_all, key_rows.shape[1]), jnp.bfloat16).at[where_to].set(key_rows)
    value_slots = jnp.zeros((slots_all, value_rows.shape[1]), jnp.bfloat16).at[where_to].set(value_rows)
    slot_doc = jnp.full((slots_all,), -1, jnp.int32).at[where_to].set(row_doc)
    scale_value = 1.0 / (HEAD_DIM ** 0.5)
    highest = lax.Precision.HIGHEST

    def one_shard(shard):
        begin = (shard * CAP).astype(jnp.int32)
        q_block = lax.dynamic_slice_in_dim(query_slots, begin, CAP, 0).astype(jnp.float32)
        k_block = lax.dynamic_slice_in_dim(key_slots, begin, CAP, 0).astype(jnp.float32)
        v_block = lax.dynamic_slice_in_dim(value_slots, begin, CAP, 0).astype(jnp.float32)
        docs_here = lax.dynamic_slice_in_dim(slot_doc, begin, CAP, 0)
        filled = docs_here >= 0
        tslots = jnp.arange(CAP)
        attend_mask = (docs_here[:, None] == docs_here[None, :]) & filled[:, None] & (tslots[None, :] <= tslots[:, None])
        q_heads = q_block.reshape(CAP, HEADS, HEAD_DIM)
        k_heads = jnp.repeat(k_block.reshape(CAP, KV_HEADS, HEAD_DIM), GROUP, axis=1)
        v_heads = jnp.repeat(v_block.reshape(CAP, KV_HEADS, HEAD_DIM), GROUP, axis=1)
        logits = jnp.einsum("thd,uhd->htu", q_heads, k_heads, precision=highest) * scale_value
        mixed = jnp.einsum("hj,htu->jtu", mix_before, logits, precision=highest)
        masked = jnp.where(attend_mask[None], mixed, -1e30)
        row_max = jnp.max(masked, axis=2, keepdims=True)
        expo_vals = jnp.where(attend_mask[None], jnp.exp(masked - row_max), 0.0)
        row_sum = jnp.sum(expo_vals, axis=2, keepdims=True)
        row_sum = jnp.where(filled[None, :, None], row_sum, 1.0)
        weights = (expo_vals / row_sum).astype(jnp.bfloat16).astype(jnp.float32)
        blended = jnp.einsum("jk,jtu->ktu", mix_after, weights, precision=highest)
        result = jnp.einsum("ktu,ukd->tkd", blended, v_heads, precision=highest)
        return result.reshape(CAP, HEADS * HEAD_DIM).astype(jnp.bfloat16)

    blocks = lax.map(one_shard, jnp.arange(N_SEQ).astype(jnp.int32))
    return blocks.reshape(N_SEQ * CAP, HEADS * HEAD_DIM)
```

```python
import functools

import jax
import jax.numpy as jnp
import numpy as np
from jax import lax
from jax.experimental import pallas as pl
from jax.experimental.pallas import tpu as pltpu
from jax.sharding import Mesh
from jax.sharding import PartitionSpec as P

THETA = 500000.0
N_SEQ = 32
HEADS = 24
GROUP = 4
HEAD_DIM = 128
KV_COLS = 32
TOK = 128
CAP = 160
PIECE = 8
META = 5
SHORT = 16
F32 = jnp.float32
BF16 = jnp.bfloat16


def iota(shape, dim):
    return lax.broadcasted_iota(jnp.int32, shape, dim)


def dot_nt(a, b):
    return lax.dot_general(a, b, (((1,), (1,)), ((), ())), preferred_element_type=F32)


def dot_nn(a, b):
    return lax.dot_general(a, b, (((1,), (0,)), ((), ())), preferred_element_type=F32)


def project_kernel(
    steps, hid, wq, wk, wv, lens, own, order, freq, send, info, acc_q, acc_kv, cos_t, sin_t, place, meta
):
    step = pl.program_id(0)
    sub = lax.axis_index("sub")

    @pl.when(step == 0)
    def _():
        shape = (TOK, TOK)
        row, col = iota(shape, 0), iota(shape, 1)
        eye = row == col
        low = row < col

        def down(value):
            return jnp.sum(jnp.where(eye, value, 0.0), axis=1, keepdims=True)

        def across(value):
            return jnp.sum(jnp.where(eye, value, 0.0), axis=0, keepdims=True)

        len_row = lens[...].astype(F32)
        own_row = own[...].astype(F32)
        len_col, own_col = down(len_row), down(own_row)
        start = jnp.sum(jnp.where(low, len_col, 0.0), axis=0, keepdims=True)
        shard_start = jnp.sum(
            jnp.where(low & (own_col == own_row), len_col, 0.0), axis=0, keepdims=True
        )
        info[...] = jnp.broadcast_to(shard_start, (8, TOK))
        packed = down(order[pl.ds(lax.axis_index("seq"), 1), :].astype(F32))
        inside = (packed >= start) & (packed < start + len_row)

        def pick(value):
            return jnp.sum(jnp.where(inside, value, 0.0), axis=1, keepdims=True)

        target = pick(own_row)
        position = packed - pick(start)
        slot = pick(shard_start) + position
        target_row = across(target)
        rank = jnp.sum(
            jnp.where((target_row == target) & (col < row), 1.0, 0.0), axis=1, keepdims=True
        )
        send_row = across(target * PIECE + rank)
        angle = position * freq[...]
        cos_t[...] = jnp.cos(angle)
        sin_t[...] = jnp.sin(angle)
        rows = iota((N_SEQ * PIECE, TOK), 0).astype(F32)
        place[:, :TOK] = jnp.where(rows == send_row, 1.0, 0.0).astype(BF16)
        place[:, TOK:] = jnp.where(rows == target_row * PIECE + META, 1.0, 0.0).astype(BF16)
        meta[...] = jnp.where(col.astype(F32) == rank, slot + 1.0, 0.0).astype(BF16)
        acc_q[...] = jnp.zeros_like(acc_q)
        acc_kv[...] = jnp.zeros_like(acc_kv)

    block = hid[...]
    acc_q[...] += dot_nn(block, wq[...])
    zero = jnp.zeros_like(wk[...])
    acc_kv[...] += dot_nt(block, jnp.concatenate([wk[...], zero, wv[...], zero], axis=0))

    @pl.when(step == steps - 1)
    def _():
        lane = iota((TOK, HEAD_DIM), 1)
        even = lane % 2 == 0
        cos_a, sin_a = cos_t[...], sin_t[...]

        def rope(value):
            partner = jnp.where(
                even, -pltpu.roll(value, HEAD_DIM - 1, 1), pltpu.roll(value, 1, 1)
            )
            return value * cos_a + partner * sin_a

        query = rope(acc_q[...]).astype(BF16)
        kv = pltpu.roll(acc_kv[...], KV_COLS * sub, 1)
        kv = jnp.where(lane // KV_COLS == sub, rope(kv), kv).astype(BF16)
        spots = place[...]
        send[:, :HEAD_DIM] = dot_nn(spots, jnp.concatenate([query, meta[...]], axis=0)).astype(BF16)
        send[:, HEAD_DIM:] = dot_nn(spots[:, :TOK], kv).astype(BF16)


def logits_kernel(scale, got, gathered, out, values):
    rows = N_SEQ * PIECE
    head = got[...].astype(F32).reshape(N_SEQ, PIECE, HEAD_DIM)
    tags = jnp.broadcast_to(head[:, META : META + 1, :], head.shape)
    hit = iota(head.shape, 2) == iota(head.shape, 1)
    slot_col = jnp.sum(jnp.where(hit, tags, 0.0), axis=2, keepdims=True).reshape(rows, 1) - 1.0
    same = iota((rows, rows), 0) == iota((rows, rows), 1)
    slot_row = jnp.sum(jnp.where(same, slot_col, 0.0), axis=0, keepdims=True)

    window = iota((rows, HEAD_DIM), 1) // KV_COLS
    key = jnp.zeros((rows, HEAD_DIM), F32)
    value = jnp.zeros((rows, HEAD_DIM), F32)
    for c in range(GROUP):
        tile = gathered[c * rows : (c + 1) * rows, :].astype(F32)
        key = jnp.where(window == c, tile, key)
        value = jnp.where(window == (c + 2) % GROUP, tile, value)
    value = pltpu.roll(value, HEAD_DIM // 2, 1)

    n = iota((rows, 1), 0)
    kv_slot = jnp.where(n < 128, n, 128 + n % 32).astype(F32)
    kv_spots = jnp.where(kv_slot == slot_row, 1.0, 0.0).astype(BF16)
    n = iota((224, 1), 0)
    late = jnp.where(n % 8 < 4, 64 + n // 8 * 4 + n % 8, -5)
    strided = 128 + 4 * (n % 8) + (n - 192) // 8
    q_slot = jnp.where(n < 128, n, jnp.where(n < 192, late, strided)).astype(F32)
    q_spots = jnp.where(q_slot == slot_row, 1.0, 0.0).astype(BF16)
    query = dot_nn(q_spots, got[...]).astype(BF16)
    key = dot_nn(kv_spots, key.astype(BF16)).astype(BF16)
    values[...] = dot_nn(kv_spots, value.astype(BF16)).astype(BF16)

    main = dot_nt(query[:192], key[:128]) * scale
    tail = dot_nt(query[192:], key[128:]) * scale
    lane = iota((8, HEAD_DIM), 1) // 32
    packed = jnp.zeros((8, HEAD_DIM), F32)
    for j in range(4):
        packed = jnp.where(lane == j, tail[8 * j : 8 * j + 8], packed)
    out[:SHORT] = main[:128].reshape(SHORT, 8, 128)
    long = main[128:].reshape(8, 8, 128)
    fifth = iota(long.shape, 1) == 4
    out[SHORT:] = jnp.where(fifth, jnp.broadcast_to(packed[:, None, :], long.shape), long)


def mix(coefs, terms, transpose):
    sums = []
    for j in range(HEADS):
        total = coefs[0, j] * terms[0]
        for h in range(1, HEADS):
            total = total + coefs[h, j] * terms[h]
        sums.append(total)
    return jnp.stack(sums)


def soften_kernel(logits, before, after, lens, own, info, out):
    owner = lax.axis_index("grp") * GROUP + lax.axis_index("sub")
    shard = lax.axis_index("seq")
    is_long = owner >= SHORT
    line = iota((8, 128), 0)
    lane = iota((8, 128), 1)
    slot = jnp.where(is_long, 128 + 4 * (owner - SHORT), 8 * owner) + line
    valid = jnp.logical_or(line < 4, jnp.logical_not(is_long))
    begin = info[...]
    length = lens[...].astype(F32)
    slot_f = slot.astype(F32)
    held = (own[...] == shard) & (slot_f >= begin) & (slot_f < begin + length) & valid
    filled = jnp.sum(jnp.where(held, 1.0, 0.0), axis=1, keepdims=True) > 0.5
    first = jnp.sum(jnp.where(held, begin, 0.0), axis=1, keepdims=True)

    def allowed(other):
        other_f = other.astype(F32)
        return (other_f >= first) & (other_f <= slot_f) & filled

    main_ok = allowed(lane)
    tail_ok = allowed(128 + lane % 32) & is_long & (lane // 32 == line)
    mixed = mix(before, [logits[h] for h in range(HEADS)], False)
    tail = jnp.broadcast_to(mixed[:, 4:5, :], mixed.shape)
    main_m = jnp.where(main_ok[None], mixed, -1e30)
    tail_m = jnp.where(tail_ok[None], tail, -1e30)
    top = jnp.max(jnp.maximum(main_m, tail_m), axis=2, keepdims=True)
    main_e = jnp.where(main_ok[None], jnp.exp(main_m - top), 0.0)
    tail_e = jnp.where(tail_ok[None], jnp.exp(tail_m - top), 0.0)
    total = jnp.sum(main_e + tail_e, axis=2, keepdims=True)
    total = jnp.where(filled[None], total, 1.0)
    main_w = (main_e / total).astype(BF16).astype(F32)
    tail_w = (tail_e / total).astype(BF16).astype(F32)
    tail_w = jnp.broadcast_to(jnp.sum(tail_w, axis=1, keepdims=True), tail_w.shape)
    weights = jnp.where(((line == 4) & is_long)[None], tail_w, main_w)
    out[...] = mix(after, [weights[h] for h in range(HEADS)], True).astype(BF16)


def output_kernel(weights, values, out):
    out[:128, :] = dot_nn(weights[:128, :], values[:128, :]).astype(BF16)
    long = weights[128:, :].astype(F32).reshape(8, 8, 128)
    tail = jnp.broadcast_to(long[:, 4:5, :], long.shape)
    tail = jnp.where(iota(long.shape, 2) // 32 == iota(long.shape, 1), tail, 0.0)
    rows = dot_nn(weights[128:, :], values[:128, :]) + dot_nn(
        tail.reshape(64, 128).astype(BF16), values[128:, :]
    )
    for i in range(8):
        out[128 + 4 * i : 132 + 4 * i, :] = rows[8 * i : 8 * i + 4, :].astype(BF16)


def on_device(
    hidden, w_query, w_key, w_value, mix_before, mix_after, doc_lengths, doc_owner, loader_order
):
    depth = hidden.shape[1]
    steps = 4
    part = depth // steps
    rows = N_SEQ * PIECE
    vmem = pl.BlockSpec(memory_space=pltpu.VMEM)
    smem = pl.BlockSpec(memory_space=pltpu.SMEM)
    pair = np.arange(HEAD_DIM) // 2
    freq = jnp.asarray((THETA ** (-2.0 * pair / HEAD_DIM)).astype(np.float32)[None, :])
    lens = doc_lengths.reshape(1, TOK)
    own = doc_owner.reshape(1, TOK)
    order = loader_order.reshape(N_SEQ, TOK)

    def whole(shape):
        return pl.BlockSpec(shape, lambda k: (0, 0))

    send, info = pl.pallas_call(
        functools.partial(project_kernel, steps),
        grid=(steps,),
        in_specs=[
            pl.BlockSpec((TOK, part), lambda k: (0, k)),
            pl.BlockSpec((part, HEAD_DIM), lambda k: (k, 0)),
            pl.BlockSpec((KV_COLS, part), lambda k: (0, k)),
            pl.BlockSpec((KV_COLS, part), lambda k: (0, k)),
            whole((1, TOK)),
            whole((1, TOK)),
            whole((N_SEQ, TOK)),
            whole((1, TOK)),
        ],
        out_specs=[whole((rows, 2 * HEAD_DIM)), whole((8, TOK))],
        out_shape=[
            jax.ShapeDtypeStruct((rows, 2 * HEAD_DIM), BF16),
            jax.ShapeDtypeStruct((8, TOK), F32),
        ],
        scratch_shapes=[
            pltpu.VMEM((TOK, HEAD_DIM), F32),
            pltpu.VMEM((TOK, HEAD_DIM), F32),
            pltpu.VMEM((TOK, HEAD_DIM), F32),
            pltpu.VMEM((TOK, HEAD_DIM), F32),
            pltpu.VMEM((rows, 2 * TOK), BF16),
            pltpu.VMEM((TOK, TOK), BF16),
        ],
        name="project",
    )(hidden, w_query, w_key.T, w_value.T, lens, own, order, freq)

    got = lax.all_to_all(
        send.reshape(N_SEQ, PIECE, 2 * HEAD_DIM), "seq", split_axis=0, concat_axis=0, tiled=True
    ).reshape(rows, 2 * HEAD_DIM)
    gathered = lax.all_gather(got[:, HEAD_DIM:], "sub", axis=0, tiled=True)

    logits, values = pl.pallas_call(
        functools.partial(logits_kernel, 1.0 / HEAD_DIM**0.5),
        in_specs=[vmem, vmem],
        out_specs=[vmem, vmem],
        out_shape=[
            jax.ShapeDtypeStruct((HEADS, 8, 128), F32),
            jax.ShapeDtypeStruct((rows, HEAD_DIM), BF16),
        ],
        name="logits",
    )(got[:, :HEAD_DIM], gathered)

    mine = lax.all_to_all(logits, ("grp", "sub"), split_axis=0, concat_axis=0, tiled=True)
    blended = pl.pallas_call(
        soften_kernel,
        in_specs=[vmem, smem, smem, vmem, vmem, vmem],
        out_specs=vmem,
        out_shape=jax.ShapeDtypeStruct((HEADS, 8, 128), BF16),
        name="soften",
    )(mine, mix_before, mix_after, lens, own, info)
    back = lax.all_to_all(blended, ("grp", "sub"), split_axis=0, concat_axis=0, tiled=True)
    return pl.pallas_call(
        output_kernel,
        in_specs=[vmem, vmem],
        out_specs=vmem,
        out_shape=jax.ShapeDtypeStruct((CAP, HEAD_DIM), BF16),
        name="output",
    )(back.reshape(HEADS * 8, 128), values)


def solution(mesh):
    split = Mesh(
        mesh.devices.reshape(N_SEQ, HEADS // GROUP, GROUP), ("seq", "grp", "sub")
    ) if not isinstance(mesh, jax.sharding.AbstractMesh) else mesh
    mp = ("grp", "sub")
    placed = (P("seq", None), P(None, mp), P(None, mp), P(None, mp), P(), P(), P(), P(), P())
    return jax.shard_map(
        on_device, mesh=split, in_specs=placed, out_specs=P("seq", mp), check_vma=False
    )
```

```python
import functools

import jax
import jax.numpy as jnp
import numpy as np
from jax import lax
from jax.experimental import pallas as pl
from jax.experimental.pallas import tpu as pltpu
from jax.sharding import Mesh
from jax.sharding import PartitionSpec as P

THETA = 500000.0
N_SEQ = 32
HEADS = 24
GROUP = 4
HEAD_DIM = 128
KV_COLS = 32
TOK = 128
CAP = 160
PIECE = 8
META = 5
SHORT = 16
F32 = jnp.float32
BF16 = jnp.bfloat16
PARTS = 4


def iota(shape, dim):
    return lax.broadcasted_iota(jnp.int32, shape, dim)


def dot_nt(a, b):
    return lax.dot_general(a, b, (((1,), (1,)), ((), ())), preferred_element_type=F32)


def dot_nn(a, b):
    return lax.dot_general(a, b, (((1,), (0,)), ((), ())), preferred_element_type=F32)


def project_kernel(
    hid_h, wq_h, wk_h, wv_h, lens_h, own_h, order_h, freq_h, send, info,
    hid, wq, wkv, lens, own, order, freq, cos_t, sin_t, place, sems,
):
    sub = lax.axis_index("sub")
    part = hid.shape[1] // PARTS
    copies = []

    def copy(source, target):
        copies.append(pltpu.make_async_copy(source, target, sems.at[len(copies)]))
        copies[-1].start()

    copy(lens_h, lens)
    copy(own_h, own)
    copy(order_h, order)
    copy(freq_h, freq)
    for k in range(PARTS):
        span = pl.ds(k * part, part)
        copy(hid_h.at[:, span], hid.at[:, span])
        copy(wq_h.at[span, :], wq.at[span, :])
        copy(wk_h.at[:, span], wkv.at[pl.ds(0, KV_COLS), span])
        copy(wv_h.at[:, span], wkv.at[pl.ds(2 * KV_COLS, KV_COLS), span])
    blank = jnp.zeros((KV_COLS, hid.shape[1]), BF16)
    wkv[KV_COLS : 2 * KV_COLS, :] = blank
    wkv[3 * KV_COLS :, :] = blank
    for k in range(4):
        copies[k].wait()

    shape = (TOK, TOK)
    row, col = iota(shape, 0), iota(shape, 1)
    eye = row == col
    low = row < col

    def down(value):
        return jnp.sum(jnp.where(eye, value, 0.0), axis=1, keepdims=True)

    def across(value):
        return jnp.sum(jnp.where(eye, value, 0.0), axis=0, keepdims=True)

    len_row = lens[...].astype(F32)
    own_row = own[...].astype(F32)
    len_col, own_col = down(len_row), down(own_row)
    start = jnp.sum(jnp.where(low, len_col, 0.0), axis=0, keepdims=True)
    shard_start = jnp.sum(
        jnp.where(low & (own_col == own_row), len_col, 0.0), axis=0, keepdims=True
    )
    info[...] = jnp.broadcast_to(shard_start, (8, TOK))
    packed = down(order[pl.ds(lax.axis_index("seq"), 1), :].astype(F32))
    inside = (packed >= start) & (packed < start + len_row)

    def pick(value):
        return jnp.sum(jnp.where(inside, value, 0.0), axis=1, keepdims=True)

    target = pick(own_row)
    position = packed - pick(start)
    slot = pick(shard_start) + position
    target_row = across(target)
    rank = jnp.sum(
        jnp.where((target_row == target) & (col < row), 1.0, 0.0), axis=1, keepdims=True
    )
    send_row = across(target * PIECE + rank)
    angle = position * freq[...]
    cos_t[...] = jnp.cos(angle)
    sin_t[...] = jnp.sin(angle)
    rows = iota((N_SEQ * PIECE, TOK), 0).astype(F32)
    place[:, :TOK] = jnp.where(rows == send_row, 1.0, 0.0).astype(BF16)
    place[:, TOK:] = jnp.where(rows == target_row * PIECE + META, 1.0, 0.0).astype(BF16)
    meta = jnp.where(col.astype(F32) == rank, slot + 1.0, 0.0).astype(BF16)

    acc_q = jnp.zeros((TOK, HEAD_DIM), F32)
    acc_kv = jnp.zeros((TOK, HEAD_DIM), F32)
    for k in range(PARTS):
        for c in copies[4 + 4 * k : 8 + 4 * k]:
            c.wait()
        block = hid[:, k * part : (k + 1) * part]
        acc_q = acc_q + dot_nn(block, wq[k * part : (k + 1) * part, :])
        acc_kv = acc_kv + dot_nt(block, wkv[:, k * part : (k + 1) * part])

    even = col % 2 == 0
    cos_a, sin_a = cos_t[...], sin_t[...]

    def rope(value):
        partner = jnp.where(even, -pltpu.roll(value, HEAD_DIM - 1, 1), pltpu.roll(value, 1, 1))
        return value * cos_a + partner * sin_a

    query = rope(acc_q).astype(BF16)
    kv = pltpu.roll(acc_kv, KV_COLS * sub, 1)
    kv = jnp.where(col // KV_COLS == sub, rope(kv), kv).astype(BF16)
    spots = place[...]
    send[:, :HEAD_DIM] = dot_nn(spots, jnp.concatenate([query, meta], axis=0)).astype(BF16)
    send[:, HEAD_DIM:] = dot_nn(spots[:, :TOK], kv).astype(BF16)


def logits_kernel(scale, got, gathered, out, values):
    rows = N_SEQ * PIECE
    mine = got[:, :HEAD_DIM]
    head = mine.astype(F32).reshape(N_SEQ, PIECE, HEAD_DIM)
    tags = jnp.broadcast_to(head[:, META : META + 1, :], head.shape)
    hit = iota(head.shape, 2) == iota(head.shape, 1)
    slot_col = jnp.sum(jnp.where(hit, tags, 0.0), axis=2, keepdims=True).reshape(rows, 1) - 1.0
    same = iota((rows, rows), 0) == iota((rows, rows), 1)
    slot_row = jnp.sum(jnp.where(same, slot_col, 0.0), axis=0, keepdims=True)

    window = iota((rows, HEAD_DIM), 1) // KV_COLS
    key = jnp.zeros((rows, HEAD_DIM), F32)
    value = jnp.zeros((rows, HEAD_DIM), F32)
    for c in range(GROUP):
        tile = gathered[c * rows : (c + 1) * rows, :].astype(F32)
        key = jnp.where(window == c, tile, key)
        value = jnp.where(window == (c + 2) % GROUP, tile, value)
    value = pltpu.roll(value, HEAD_DIM // 2, 1)

    n = iota((rows, 1), 0)
    kv_slot = jnp.where(n < 128, n, 128 + n % 32).astype(F32)
    kv_spots = jnp.where(kv_slot == slot_row, 1.0, 0.0).astype(BF16)
    n = iota((224, 1), 0)
    late = jnp.where(n % 8 < 4, 64 + n // 8 * 4 + n % 8, -5)
    strided = 128 + 4 * (n % 8) + (n - 192) // 8
    q_slot = jnp.where(n < 128, n, jnp.where(n < 192, late, strided)).astype(F32)
    q_spots = jnp.where(q_slot == slot_row, 1.0, 0.0).astype(BF16)
    query = dot_nn(q_spots, mine).astype(BF16)
    key = dot_nn(kv_spots, key.astype(BF16)).astype(BF16)
    values[...] = dot_nn(kv_spots, value.astype(BF16)).astype(BF16)

    main = dot_nt(query[:192], key[:128]) * scale
    tail = dot_nt(query[192:], key[128:]) * scale
    lane = iota((8, HEAD_DIM), 1) // 32
    packed = jnp.zeros((8, HEAD_DIM), F32)
    for j in range(4):
        packed = jnp.where(lane == j, tail[8 * j : 8 * j + 8], packed)
    out[:SHORT] = main[:128].reshape(SHORT, 8, 128)
    long = main[128:].reshape(8, 8, 128)
    fifth = iota(long.shape, 1) == 4
    out[SHORT:] = jnp.where(fifth, jnp.broadcast_to(packed[:, None, :], long.shape), long)


def mix(coefs, terms):
    sums = []
    for j in range(HEADS):
        total = coefs[0, j] * terms[0]
        for h in range(1, HEADS):
            total = total + coefs[h, j] * terms[h]
        sums.append(total)
    return jnp.stack(sums)


def soften_kernel(logits, before, after, lens, own, info, out):
    owner = lax.axis_index("grp") * GROUP + lax.axis_index("sub")
    shard = lax.axis_index("seq")
    is_long = owner >= SHORT
    line = iota((8, 128), 0)
    lane = iota((8, 128), 1)
    slot = jnp.where(is_long, 128 + 4 * (owner - SHORT), 8 * owner) + line
    valid = jnp.logical_or(line < 4, jnp.logical_not(is_long))
    begin = info[...]
    length = lens[...].astype(F32)
    slot_f = slot.astype(F32)
    held = (own[...] == shard) & (slot_f >= begin) & (slot_f < begin + length) & valid
    filled = jnp.sum(jnp.where(held, 1.0, 0.0), axis=1, keepdims=True) > 0.5
    first = jnp.sum(jnp.where(held, begin, 0.0), axis=1, keepdims=True)

    def allowed(other):
        other_f = other.astype(F32)
        return (other_f >= first) & (other_f <= slot_f) & filled

    main_ok = allowed(lane)
    tail_ok = allowed(128 + lane % 32) & is_long & (lane // 32 == line)
    mixed = mix(before, [logits[h] for h in range(HEADS)])
    tail = jnp.broadcast_to(mixed[:, 4:5, :], mixed.shape)
    main_m = jnp.where(main_ok[None], mixed, -1e30)
    tail_m = jnp.where(tail_ok[None], tail, -1e30)
    top = jnp.max(jnp.maximum(main_m, tail_m), axis=2, keepdims=True)
    main_e = jnp.where(main_ok[None], jnp.exp(main_m - top), 0.0)
    tail_e = jnp.where(tail_ok[None], jnp.exp(tail_m - top), 0.0)
    total = jnp.sum(main_e + tail_e, axis=2, keepdims=True)
    total = jnp.where(filled[None], total, 1.0)
    main_w = (main_e / total).astype(BF16).astype(F32)
    tail_w = (tail_e / total).astype(BF16).astype(F32)
    tail_w = jnp.broadcast_to(jnp.sum(tail_w, axis=1, keepdims=True), tail_w.shape)
    weights = jnp.where(((line == 4) & is_long)[None], tail_w, main_w)
    out[...] = mix(after, [weights[h] for h in range(HEADS)]).astype(BF16)


def output_kernel(weights, values, out):
    out[:128, :] = dot_nn(weights[:128, :], values[:128, :]).astype(BF16)
    long = weights[128:, :].astype(F32).reshape(8, 8, 128)
    tail = jnp.broadcast_to(long[:, 4:5, :], long.shape)
    tail = jnp.where(iota(long.shape, 2) // 32 == iota(long.shape, 1), tail, 0.0)
    rows = dot_nn(weights[128:, :], values[:128, :]) + dot_nn(
        tail.reshape(64, 128).astype(BF16), values[128:, :]
    )
    for i in range(8):
        out[128 + 4 * i : 132 + 4 * i, :] = rows[8 * i : 8 * i + 4, :].astype(BF16)


def on_device(
    hidden, w_query, w_key, w_value, mix_before, mix_after, doc_lengths, doc_owner, loader_order
):
    depth = hidden.shape[1]
    grant = pltpu.CompilerParams(vmem_limit_bytes=12 << 20)
    rows = N_SEQ * PIECE
    vmem = pl.BlockSpec(memory_space=pltpu.VMEM)
    smem = pl.BlockSpec(memory_space=pltpu.SMEM)
    pair = np.arange(HEAD_DIM) // 2
    freq = jnp.asarray((THETA ** (-2.0 * pair / HEAD_DIM)).astype(np.float32)[None, :])
    lens = doc_lengths.reshape(1, TOK)
    own = doc_owner.reshape(1, TOK)
    order = loader_order.reshape(N_SEQ, TOK)

    hbm = pl.BlockSpec(memory_space=pltpu.HBM)
    send, info = pl.pallas_call(
        project_kernel,
        in_specs=[hbm] * 8,
        out_specs=[vmem, vmem],
        out_shape=[
            jax.ShapeDtypeStruct((rows, 2 * HEAD_DIM), BF16),
            jax.ShapeDtypeStruct((8, TOK), F32),
        ],
        scratch_shapes=[
            pltpu.VMEM((TOK, depth), BF16),
            pltpu.VMEM((depth, HEAD_DIM), BF16),
            pltpu.VMEM((4 * KV_COLS, depth), BF16),
            pltpu.VMEM((1, TOK), jnp.int32),
            pltpu.VMEM((1, TOK), jnp.int32),
            pltpu.VMEM((N_SEQ, TOK), jnp.int32),
            pltpu.VMEM((1, TOK), F32),
            pltpu.VMEM((TOK, HEAD_DIM), F32),
            pltpu.VMEM((TOK, HEAD_DIM), F32),
            pltpu.VMEM((rows, 2 * TOK), BF16),
            pltpu.SemaphoreType.DMA((4 + 4 * PARTS,)),
        ],
        compiler_params=grant,
        name="project",
    )(
        *[
            pltpu.with_memory_space_constraint(x, pltpu.HBM)
            for x in (hidden, w_query, w_key.T, w_value.T, lens, own, order, freq)
        ]
    )

    got = lax.all_to_all(
        send.reshape(N_SEQ, PIECE, 2 * HEAD_DIM), "seq", split_axis=0, concat_axis=0, tiled=True
    ).reshape(rows, 2 * HEAD_DIM)
    gathered = lax.all_gather(got[:, HEAD_DIM:], "sub", axis=0, tiled=True)

    logits, values = pl.pallas_call(
        functools.partial(logits_kernel, 1.0 / HEAD_DIM**0.5),
        in_specs=[vmem, vmem],
        out_specs=[vmem, vmem],
        out_shape=[
            jax.ShapeDtypeStruct((HEADS, 8, 128), F32),
            jax.ShapeDtypeStruct((rows, HEAD_DIM), BF16),
        ],
        compiler_params=grant,
        name="logits",
    )(got, gathered)

    mine = lax.all_to_all(logits, ("grp", "sub"), split_axis=0, concat_axis=0, tiled=True)
    blended = pl.pallas_call(
        soften_kernel,
        in_specs=[vmem, smem, smem, vmem, vmem, vmem],
        out_specs=vmem,
        out_shape=jax.ShapeDtypeStruct((HEADS, 8, 128), BF16),
        compiler_params=grant,
        name="soften",
    )(mine, mix_before, mix_after, lens, own, info)
    back = lax.all_to_all(blended, ("grp", "sub"), split_axis=0, concat_axis=0, tiled=True)
    return pl.pallas_call(
        output_kernel,
        in_specs=[vmem, vmem],
        out_specs=vmem,
        out_shape=jax.ShapeDtypeStruct((CAP, HEAD_DIM), BF16),
        compiler_params=grant,
        name="output",
    )(back.reshape(HEADS * 8, 128), values)


def solution(mesh):
    split = Mesh(
        mesh.devices.reshape(N_SEQ, HEADS // GROUP, GROUP), ("seq", "grp", "sub")
    ) if not isinstance(mesh, jax.sharding.AbstractMesh) else mesh
    mp = ("grp", "sub")
    placed = (P("seq", None), P(None, mp), P(None, mp), P(None, mp), P(), P(), P(), P(), P())
    return jax.shard_map(
        on_device, mesh=split, in_specs=placed, out_specs=P("seq", mp), check_vma=False
    )
```

```python
import functools

import jax
import jax.numpy as jnp
import numpy as np
from jax import lax
from jax.experimental import pallas as pl
from jax.experimental.pallas import tpu as pltpu
from jax.sharding import Mesh
from jax.sharding import PartitionSpec as P

THETA = 500000.0
N_SEQ = 32
HEADS = 24
GROUP = 4
HEAD_DIM = 128
KV_COLS = 32
TOK = 128
CAP = 160
PIECE = 8
META = 5
SHORT = 16
F32 = jnp.float32
BF16 = jnp.bfloat16
PARTS = 1


def iota(shape, dim):
    return lax.broadcasted_iota(jnp.int32, shape, dim)


def dot_nt(a, b):
    return lax.dot_general(a, b, (((1,), (1,)), ((), ())), preferred_element_type=F32)


def dot_nn(a, b):
    return lax.dot_general(a, b, (((1,), (0,)), ((), ())), preferred_element_type=F32)


def project_kernel(
    hid_h, wq_h, wk_h, wv_h, lens_h, own_h, order_h, freq_h, send, info,
    hid, wq, wkv, lens, own, order, freq, cos_t, sin_t, place, sems,
):
    sub = lax.axis_index("sub")
    part = hid.shape[1] // PARTS
    copies = []

    def copy(source, target):
        copies.append(pltpu.make_async_copy(source, target, sems.at[len(copies)]))
        copies[-1].start()

    copy(lens_h, lens)
    copy(own_h, own)
    copy(order_h, order)
    copy(freq_h, freq)
    for k in range(PARTS):
        span = pl.ds(k * part, part)
        copy(hid_h.at[:, span], hid.at[:, span])
        copy(wq_h.at[span, :], wq.at[span, :])
        copy(wk_h.at[:, span], wkv.at[pl.ds(0, KV_COLS), span])
        copy(wv_h.at[:, span], wkv.at[pl.ds(2 * KV_COLS, KV_COLS), span])
    blank = jnp.zeros((KV_COLS, hid.shape[1]), BF16)
    wkv[KV_COLS : 2 * KV_COLS, :] = blank
    wkv[3 * KV_COLS :, :] = blank
    for k in range(4):
        copies[k].wait()

    shape = (TOK, TOK)
    row, col = iota(shape, 0), iota(shape, 1)
    eye = row == col
    low = row < col

    def down(value):
        return jnp.sum(jnp.where(eye, value, 0.0), axis=1, keepdims=True)

    def across(value):
        return jnp.sum(jnp.where(eye, value, 0.0), axis=0, keepdims=True)

    len_row = lens[...].astype(F32)
    own_row = own[...].astype(F32)
    len_col, own_col = down(len_row), down(own_row)
    start = jnp.sum(jnp.where(low, len_col, 0.0), axis=0, keepdims=True)
    shard_start = jnp.sum(
        jnp.where(low & (own_col == own_row), len_col, 0.0), axis=0, keepdims=True
    )
    line = iota((8, TOK), 0)
    info[...] = jnp.where(line == 0, shard_start, jnp.where(line == 1, len_row, own_row))
    packed = down(order[pl.ds(lax.axis_index("seq"), 1), :].astype(F32))
    inside = (packed >= start) & (packed < start + len_row)

    def pick(value):
        return jnp.sum(jnp.where(inside, value, 0.0), axis=1, keepdims=True)

    target = pick(own_row)
    position = packed - pick(start)
    slot = pick(shard_start) + position
    target_row = across(target)
    rank = jnp.sum(
        jnp.where((target_row == target) & (col < row), 1.0, 0.0), axis=1, keepdims=True
    )
    send_row = across(target * PIECE + rank)
    angle = position * freq[...]
    cos_t[...] = jnp.cos(angle)
    sin_t[...] = jnp.sin(angle)
    rows = iota((N_SEQ * PIECE, TOK), 0).astype(F32)
    place[:, :TOK] = jnp.where(rows == send_row, 1.0, 0.0).astype(BF16)
    place[:, TOK:] = jnp.where(rows == target_row * PIECE + META, 1.0, 0.0).astype(BF16)
    meta = jnp.where(col.astype(F32) == rank, slot + 1.0, 0.0).astype(BF16)

    acc_q = jnp.zeros((TOK, HEAD_DIM), F32)
    acc_kv = jnp.zeros((TOK, HEAD_DIM), F32)
    for k in range(PARTS):
        for c in copies[4 + 4 * k : 8 + 4 * k]:
            c.wait()
        block = hid[:, k * part : (k + 1) * part]
        acc_q = acc_q + dot_nn(block, wq[k * part : (k + 1) * part, :])
        acc_kv = acc_kv + dot_nt(block, wkv[:, k * part : (k + 1) * part])

    even = col % 2 == 0
    cos_a, sin_a = cos_t[...], sin_t[...]

    def rope(value):
        partner = jnp.where(even, -pltpu.roll(value, HEAD_DIM - 1, 1), pltpu.roll(value, 1, 1))
        return value * cos_a + partner * sin_a

    query = rope(acc_q).astype(BF16)
    kv = pltpu.roll(acc_kv, KV_COLS * sub, 1)
    kv = jnp.where(col // KV_COLS == sub, rope(kv), kv).astype(BF16)
    spots = place[...]
    send[:, :HEAD_DIM] = dot_nn(spots, jnp.concatenate([query, meta], axis=0)).astype(BF16)
    send[:, HEAD_DIM:] = dot_nn(spots[:, :TOK], kv).astype(BF16)


def logits_kernel(scale, got, gathered, out, values):
    rows = N_SEQ * PIECE
    mine = got[:, :HEAD_DIM]
    head = mine.astype(F32).reshape(N_SEQ, PIECE, HEAD_DIM)
    tags = jnp.broadcast_to(head[:, META : META + 1, :], head.shape)
    hit = iota(head.shape, 2) == iota(head.shape, 1)
    slot_col = jnp.sum(jnp.where(hit, tags, 0.0), axis=2, keepdims=True).reshape(rows, 1) - 1.0
    same = iota((rows, rows), 0) == iota((rows, rows), 1)
    slot_row = jnp.sum(jnp.where(same, slot_col, 0.0), axis=0, keepdims=True)

    window = iota((rows, HEAD_DIM), 1) // KV_COLS
    key = jnp.zeros((rows, HEAD_DIM), F32)
    value = jnp.zeros((rows, HEAD_DIM), F32)
    for c in range(GROUP):
        tile = gathered[c * rows : (c + 1) * rows, :].astype(F32)
        key = jnp.where(window == c, tile, key)
        value = jnp.where(window == (c + 2) % GROUP, tile, value)
    value = pltpu.roll(value, HEAD_DIM // 2, 1)

    n = iota((rows, 1), 0)
    kv_slot = jnp.where(n < 128, n, 128 + n % 32).astype(F32)
    kv_spots = jnp.where(kv_slot == slot_row, 1.0, 0.0).astype(BF16)
    n = iota((224, 1), 0)
    late = jnp.where(n % 8 < 4, 64 + n // 8 * 4 + n % 8, -5)
    strided = 128 + 4 * (n % 8) + (n - 192) // 8
    q_slot = jnp.where(n < 128, n, jnp.where(n < 192, late, strided)).astype(F32)
    q_spots = jnp.where(q_slot == slot_row, 1.0, 0.0).astype(BF16)
    query = dot_nn(q_spots, mine).astype(BF16)
    key = dot_nn(kv_spots, key.astype(BF16)).astype(BF16)
    values[...] = dot_nn(kv_spots, value.astype(BF16)).astype(BF16)

    main = dot_nt(query[:192], key[:128]) * scale
    tail = dot_nt(query[192:], key[128:]) * scale
    lane = iota((8, HEAD_DIM), 1) // 32
    packed = jnp.zeros((8, HEAD_DIM), F32)
    for j in range(4):
        packed = jnp.where(lane == j, tail[8 * j : 8 * j + 8], packed)
    out[:SHORT] = main[:128].reshape(SHORT, 8, 128)
    long = main[128:].reshape(8, 8, 128)
    fifth = iota(long.shape, 1) == 4
    out[SHORT:] = jnp.where(fifth, jnp.broadcast_to(packed[:, None, :], long.shape), long)


def spread(coefs, table):
    for j in range(HEADS):
        table[j] = jnp.broadcast_to(coefs[:, j : j + 1], (HEADS, 128))


def mix(table, terms):
    sums = []
    for j in range(HEADS):
        total = table[j, 0:1, :] * terms[0]
        for h in range(1, HEADS):
            total = total + table[j, h : h + 1, :] * terms[h]
        sums.append(total)
    return jnp.stack(sums)


def soften_kernel(logits, before, after, info, out, table_b, table_a):
    owner = lax.axis_index("grp") * GROUP + lax.axis_index("sub")
    shard = lax.axis_index("seq").astype(F32)
    spread(before, table_b)
    spread(after, table_a)
    is_long = owner >= SHORT
    line = iota((8, 128), 0)
    lane = iota((8, 128), 1)
    slot = jnp.where(is_long, 128 + 4 * (owner - SHORT), 8 * owner) + line
    valid = jnp.logical_or(line < 4, jnp.logical_not(is_long))
    begin, length, own = info[0:1, :], info[1:2, :], info[2:3, :]
    slot_f = slot.astype(F32)
    held = (own == shard) & (slot_f >= begin) & (slot_f < begin + length) & valid
    filled = jnp.sum(jnp.where(held, 1.0, 0.0), axis=1, keepdims=True) > 0.5
    first = jnp.sum(jnp.where(held, begin, 0.0), axis=1, keepdims=True)

    def allowed(other):
        other_f = other.astype(F32)
        return (other_f >= first) & (other_f <= slot_f) & filled

    main_ok = allowed(lane)
    tail_ok = allowed(128 + lane % 32) & is_long & (lane // 32 == line)
    mixed = mix(table_b, [logits[h] for h in range(HEADS)])
    tail = jnp.broadcast_to(mixed[:, 4:5, :], mixed.shape)
    main_m = jnp.where(main_ok[None], mixed, -1e30)
    tail_m = jnp.where(tail_ok[None], tail, -1e30)
    top = jnp.max(jnp.maximum(main_m, tail_m), axis=2, keepdims=True)
    main_e = jnp.where(main_ok[None], jnp.exp(main_m - top), 0.0)
    tail_e = jnp.where(tail_ok[None], jnp.exp(tail_m - top), 0.0)
    total = jnp.sum(main_e + tail_e, axis=2, keepdims=True)
    share = 1.0 / jnp.where(filled[None], total, 1.0)
    main_w = (main_e * share).astype(BF16).astype(F32)
    tail_w = (tail_e * share).astype(BF16).astype(F32)
    tail_w = jnp.broadcast_to(jnp.sum(tail_w, axis=1, keepdims=True), tail_w.shape)
    weights = jnp.where(((line == 4) & is_long)[None], tail_w, main_w)
    out[...] = mix(table_a, [weights[h] for h in range(HEADS)]).astype(BF16)


def output_kernel(weights, values, out):
    out[:128, :] = dot_nn(weights[:128, :], values[:128, :]).astype(BF16)
    long = weights[128:, :].astype(F32).reshape(8, 8, 128)
    tail = jnp.broadcast_to(long[:, 4:5, :], long.shape)
    tail = jnp.where(iota(long.shape, 2) // 32 == iota(long.shape, 1), tail, 0.0)
    rows = dot_nn(weights[128:, :], values[:128, :]) + dot_nn(
        tail.reshape(64, 128).astype(BF16), values[128:, :]
    )
    for i in range(8):
        out[128 + 4 * i : 132 + 4 * i, :] = rows[8 * i : 8 * i + 4, :].astype(BF16)


def on_device(
    hidden, w_query, w_key, w_value, mix_before, mix_after, doc_lengths, doc_owner, loader_order
):
    depth = hidden.shape[1]
    grant = pltpu.CompilerParams(vmem_limit_bytes=12 << 20)
    rows = N_SEQ * PIECE
    vmem = pl.BlockSpec(memory_space=pltpu.VMEM)
    pair = np.arange(HEAD_DIM) // 2
    freq = jnp.asarray((THETA ** (-2.0 * pair / HEAD_DIM)).astype(np.float32)[None, :])
    lens = doc_lengths.reshape(1, TOK)
    own = doc_owner.reshape(1, TOK)
    order = loader_order.reshape(N_SEQ, TOK)

    hbm = pl.BlockSpec(memory_space=pltpu.HBM)
    send, info = pl.pallas_call(
        project_kernel,
        in_specs=[hbm] * 8,
        out_specs=[vmem, vmem],
        out_shape=[
            jax.ShapeDtypeStruct((rows, 2 * HEAD_DIM), BF16),
            jax.ShapeDtypeStruct((8, TOK), F32),
        ],
        scratch_shapes=[
            pltpu.VMEM((TOK, depth), BF16),
            pltpu.VMEM((depth, HEAD_DIM), BF16),
            pltpu.VMEM((4 * KV_COLS, depth), BF16),
            pltpu.VMEM((1, TOK), jnp.int32),
            pltpu.VMEM((1, TOK), jnp.int32),
            pltpu.VMEM((N_SEQ, TOK), jnp.int32),
            pltpu.VMEM((1, TOK), F32),
            pltpu.VMEM((TOK, HEAD_DIM), F32),
            pltpu.VMEM((TOK, HEAD_DIM), F32),
            pltpu.VMEM((rows, 2 * TOK), BF16),
            pltpu.SemaphoreType.DMA((4 + 4 * PARTS,)),
        ],
        compiler_params=grant,
        name="project",
    )(
        *[
            pltpu.with_memory_space_constraint(x, pltpu.HBM)
            for x in (hidden, w_query, w_key.T, w_value.T, lens, own, order, freq)
        ]
    )

    got = lax.all_to_all(
        send.reshape(N_SEQ, PIECE, 2 * HEAD_DIM), "seq", split_axis=0, concat_axis=0, tiled=True
    ).reshape(rows, 2 * HEAD_DIM)
    gathered = lax.all_gather(got[:, HEAD_DIM:], "sub", axis=0, tiled=True)

    logits, values = pl.pallas_call(
        functools.partial(logits_kernel, 1.0 / HEAD_DIM**0.5),
        in_specs=[vmem, vmem],
        out_specs=[vmem, vmem],
        out_shape=[
            jax.ShapeDtypeStruct((HEADS, 8, 128), F32),
            jax.ShapeDtypeStruct((rows, HEAD_DIM), BF16),
        ],
        compiler_params=grant,
        name="logits",
    )(got, gathered)

    mine = lax.all_to_all(logits, ("grp", "sub"), split_axis=0, concat_axis=0, tiled=True)
    blended = pl.pallas_call(
        soften_kernel,
        in_specs=[vmem] * 4,
        out_specs=vmem,
        out_shape=jax.ShapeDtypeStruct((HEADS, 8, 128), BF16),
        scratch_shapes=[pltpu.VMEM((HEADS, HEADS, 128), F32)] * 2,
        compiler_params=grant,
        name="soften",
    )(mine, mix_before, mix_after, info)
    back = lax.all_to_all(blended, ("grp", "sub"), split_axis=0, concat_axis=0, tiled=True)
    return pl.pallas_call(
        output_kernel,
        in_specs=[vmem, vmem],
        out_specs=vmem,
        out_shape=jax.ShapeDtypeStruct((CAP, HEAD_DIM), BF16),
        compiler_params=grant,
        name="output",
    )(back.reshape(HEADS * 8, 128), values)


def solution(mesh):
    split = Mesh(
        mesh.devices.reshape(N_SEQ, HEADS // GROUP, GROUP), ("seq", "grp", "sub")
    ) if not isinstance(mesh, jax.sharding.AbstractMesh) else mesh
    mp = ("grp", "sub")
    placed = (P("seq", None), P(None, mp), P(None, mp), P(None, mp), P(), P(), P(), P(), P())
    return jax.shard_map(
        on_device, mesh=split, in_specs=placed, out_specs=P("seq", mp), check_vma=False
    )
```

```python
import functools

import jax
import jax.numpy as jnp
import numpy as np
from jax import lax
from jax.experimental import pallas as pl
from jax.experimental.pallas import tpu as pltpu
from jax.sharding import Mesh
from jax.sharding import PartitionSpec as P

THETA = 500000.0
N_SEQ = 32
HEADS = 24
GROUP = 4
HEAD_DIM = 128
KV_COLS = 32
TOK = 128
CAP = 160
PIECE = 8
KV_ROW = 5
META = 7
SHORT = 16
F32 = jnp.float32
BF16 = jnp.bfloat16


def iota(shape, dim):
    return lax.broadcasted_iota(jnp.int32, shape, dim)


def dot_nt(a, b):
    return lax.dot_general(a, b, (((1,), (1,)), ((), ())), preferred_element_type=F32)


def dot_nn(a, b):
    return lax.dot_general(a, b, (((1,), (0,)), ((), ())), preferred_element_type=F32)


def turn(shape, sub):
    return (iota(shape, len(shape) - 1) - KV_COLS * sub) & (HEAD_DIM - 1)


def project_kernel(
    hid_h, wq_h, wk_h, wv_h, lens_h, own_h, order_h, freq_h, send, info,
    hid, wq, wkv, lens, own, order, freq, cos_t, sin_t, place, sems,
):
    sub = lax.axis_index("sub")
    copies = []

    def copy(source, target):
        copies.append(pltpu.make_async_copy(source, target, sems.at[len(copies)]))
        copies[-1].start()

    copy(lens_h, lens)
    copy(own_h, own)
    copy(order_h, order)
    copy(freq_h, freq)
    copy(hid_h, hid)
    copy(wq_h, wq)
    copy(wk_h, wkv.at[pl.ds(0, KV_COLS), :])
    copy(wv_h, wkv.at[pl.ds(KV_COLS, KV_COLS), :])
    wkv[2 * KV_COLS :, :] = jnp.zeros((2 * KV_COLS, hid.shape[1]), BF16)
    for k in range(4):
        copies[k].wait()

    shape = (TOK, TOK)
    row, col = iota(shape, 0), iota(shape, 1)
    eye = row == col
    low = row < col

    def down(value):
        return jnp.sum(jnp.where(eye, value, 0.0), axis=1, keepdims=True)

    def across(value):
        return jnp.sum(jnp.where(eye, value, 0.0), axis=0, keepdims=True)

    len_row = lens[...].astype(F32)
    own_row = own[...].astype(F32)
    len_col, own_col = down(len_row), down(own_row)
    start = jnp.sum(jnp.where(low, len_col, 0.0), axis=0, keepdims=True)
    shard_start = jnp.sum(
        jnp.where(low & (own_col == own_row), len_col, 0.0), axis=0, keepdims=True
    )
    line = iota((8, TOK), 0)
    info[...] = jnp.where(line == 0, shard_start, jnp.where(line == 1, len_row, own_row))
    packed = down(order[pl.ds(lax.axis_index("seq"), 1), :].astype(F32))
    inside = (packed >= start) & (packed < start + len_row)

    def pick(value):
        return jnp.sum(jnp.where(inside, value, 0.0), axis=1, keepdims=True)

    target = pick(own_row)
    position = packed - pick(start)
    slot = pick(shard_start) + position
    target_row = across(target)
    rank = jnp.sum(
        jnp.where((target_row == target) & (col < row), 1.0, 0.0), axis=1, keepdims=True
    )
    pair = jnp.floor(rank * 0.5)
    angle = position * freq[...]
    cos_t[...] = jnp.cos(angle)
    sin_t[...] = jnp.sin(angle)
    rows = iota((N_SEQ * PIECE, TOK), 0).astype(F32)

    def put(k, where_to):
        place[:, k * TOK : (k + 1) * TOK] = jnp.where(rows == where_to, 1.0, 0.0).astype(BF16)

    put(0, across(target * PIECE + rank))
    put(1, across(target * PIECE + KV_ROW + pair))
    put(2, target_row * PIECE + META)
    turned = turn(shape, sub)
    meta = turned.astype(F32) == rank + HEAD_DIM // 2
    meta = jnp.where(meta, slot + 1.0, 0.0).astype(BF16)
    side = (turned // (HEAD_DIM // 2)).astype(F32) == rank - 2.0 * pair

    for c in copies[4:]:
        c.wait()
    acc_q = dot_nn(hid[...], wq[...])
    acc_kv = dot_nt(hid[...], wkv[...])
    even = col % 2 == 0

    cos_a, sin_a = cos_t[...], sin_t[...]

    def rope(value):
        partner = jnp.where(even, -pltpu.roll(value, HEAD_DIM - 1, 1), pltpu.roll(value, 1, 1))
        return value * cos_a + partner * sin_a

    query = rope(acc_q).astype(BF16)
    kv = pltpu.roll(acc_kv, KV_COLS * sub, 1)
    kv = jnp.where(turned < KV_COLS, rope(kv), kv)
    kv = jnp.where(side, kv + pltpu.roll(kv, HEAD_DIM // 2, 1), 0.0).astype(BF16)
    send[...] = dot_nn(place[...], jnp.concatenate([query, kv, meta], axis=0)).astype(BF16)


def logits_kernel(scale, got, gathered, out, values):
    rows = N_SEQ * PIECE
    mine = got[...]
    head = mine.astype(F32).reshape(N_SEQ, PIECE, HEAD_DIM)
    tags = jnp.broadcast_to(head[:, META : META + 1, :], head.shape)
    line, lane = iota(head.shape, 1), turn(head.shape, lax.axis_index("sub")) - HEAD_DIM // 2
    same = iota((rows, rows), 0) == iota((rows, rows), 1)

    token = jnp.where(line < KV_ROW, line, 2 * (line - KV_ROW))
    weight = jnp.where((lane == token + 1) & (line >= KV_ROW) & (line < META), 256.0, 0.0)
    weight = jnp.where(lane == token, 1.0, weight)
    column = jnp.sum(weight * tags, axis=2, keepdims=True).reshape(rows, 1)
    both = jnp.sum(jnp.where(same, column, 0.0), axis=0, keepdims=True)
    right = jnp.floor(both * (1.0 / 256.0))
    left, right = both - 256.0 * right - 1.0, right - 1.0
    is_query = iota((1, rows), 1) % PIECE < KV_ROW

    window = iota((rows, HEAD_DIM), 1) // KV_COLS
    blocks = [jnp.zeros((rows, HEAD_DIM), F32)] * 4
    for c in range(GROUP):
        tile = gathered[c * rows : (c + 1) * rows, :].astype(F32)
        for i in range(4):
            blocks[i] = jnp.where(window == (c + i) % GROUP, tile, blocks[i])
    for i in range(1, 4):
        blocks[i] = pltpu.roll(blocks[i], HEAD_DIM - i * KV_COLS, 1)
    key = jnp.concatenate([blocks[0].astype(BF16), blocks[2].astype(BF16)], axis=0)
    value = jnp.concatenate([blocks[1].astype(BF16), blocks[3].astype(BF16)], axis=0)

    n = iota((rows, 1), 0)
    kv_slot = jnp.where(n < 128, n, 128 + n % 32).astype(F32)
    from_left = jnp.where(kv_slot == jnp.where(is_query, -1.0, left), 1.0, 0.0).astype(BF16)
    from_right = jnp.where(kv_slot == right, 1.0, 0.0).astype(BF16)
    kv_spots = jnp.concatenate([from_left, from_right], axis=1)
    n = iota((224, 1), 0)
    late = jnp.where(n % 8 < 4, 64 + n // 8 * 4 + n % 8, -5)
    strided = 128 + 4 * (n % 8) + (n - 192) // 8
    q_slot = jnp.where(n < 128, n, jnp.where(n < 192, late, strided)).astype(F32)
    q_spots = jnp.where(q_slot == jnp.where(is_query, left, -1.0), 1.0, 0.0).astype(BF16)
    query = dot_nn(q_spots, mine).astype(BF16)
    key = dot_nn(kv_spots, key).astype(BF16)
    values[...] = dot_nn(kv_spots, value).astype(BF16)

    main = dot_nt(query[:192], key[:128]) * scale
    tail = dot_nt(query[192:], key[128:]) * scale
    lane = iota((8, HEAD_DIM), 1) // 32
    packed = jnp.zeros((8, HEAD_DIM), F32)
    for j in range(4):
        packed = jnp.where(lane == j, tail[8 * j : 8 * j + 8], packed)
    out[:SHORT] = main[:128].reshape(SHORT, 8, 128)
    long = main[128:].reshape(8, 8, 128)
    fifth = iota(long.shape, 1) == 4
    out[SHORT:] = jnp.where(fifth, jnp.broadcast_to(packed[:, None, :], long.shape), long)


def spread(coefs, table):
    for j in range(HEADS):
        table[j] = jnp.broadcast_to(coefs[:, j : j + 1], (HEADS, 128))


def mix(table, terms):
    sums = []
    for j in range(HEADS):
        total = table[j, 0:1, :] * terms[0]
        for h in range(1, HEADS):
            total = total + table[j, h : h + 1, :] * terms[h]
        sums.append(total)
    return jnp.stack(sums)


def soften_kernel(logits, before, after, info, out, table_b, table_a):
    owner = lax.axis_index("grp") * GROUP + lax.axis_index("sub")
    shard = lax.axis_index("seq").astype(F32)
    spread(before, table_b)
    spread(after, table_a)
    is_long = owner >= SHORT
    line = iota((8, 128), 0)
    lane = iota((8, 128), 1)
    slot = jnp.where(is_long, 128 + 4 * (owner - SHORT), 8 * owner) + line
    valid = jnp.logical_or(line < 4, jnp.logical_not(is_long))
    begin, length, own = info[0:1, :], info[1:2, :], info[2:3, :]
    slot_f = slot.astype(F32)
    held = (own == shard) & (slot_f >= begin) & (slot_f < begin + length) & valid
    filled = jnp.sum(jnp.where(held, 1.0, 0.0), axis=1, keepdims=True) > 0.5
    first = jnp.sum(jnp.where(held, begin, 0.0), axis=1, keepdims=True)

    def allowed(other):
        other_f = other.astype(F32)
        return (other_f >= first) & (other_f <= slot_f) & filled

    main_ok = allowed(lane)
    tail_ok = allowed(128 + lane % 32) & is_long & (lane // 32 == line)
    mixed = mix(table_b, [logits[h] for h in range(HEADS)])
    tail = jnp.broadcast_to(mixed[:, 4:5, :], mixed.shape)
    main_m = jnp.where(main_ok[None], mixed, -1e30)
    tail_m = jnp.where(tail_ok[None], tail, -1e30)
    top = jnp.max(jnp.maximum(main_m, tail_m), axis=2, keepdims=True)
    main_e = jnp.where(main_ok[None], jnp.exp(main_m - top), 0.0)
    tail_e = jnp.where(tail_ok[None], jnp.exp(tail_m - top), 0.0)
    total = jnp.sum(main_e + tail_e, axis=2, keepdims=True)
    share = 1.0 / jnp.where(filled[None], total, 1.0)
    main_w = (main_e * share).astype(BF16).astype(F32)
    tail_w = (tail_e * share).astype(BF16).astype(F32)
    tail_w = jnp.broadcast_to(jnp.sum(tail_w, axis=1, keepdims=True), tail_w.shape)
    weights = jnp.where(((line == 4) & is_long)[None], tail_w, main_w)
    out[...] = mix(table_a, [weights[h] for h in range(HEADS)]).astype(BF16)


def output_kernel(weights, values, out):
    out[:128, :] = dot_nn(weights[:128, :], values[:128, :]).astype(BF16)
    long = weights[128:, :].astype(F32).reshape(8, 8, 128)
    tail = jnp.broadcast_to(long[:, 4:5, :], long.shape)
    tail = jnp.where(iota(long.shape, 2) // 32 == iota(long.shape, 1), tail, 0.0)
    rows = dot_nn(weights[128:, :], values[:128, :]) + dot_nn(
        tail.reshape(64, 128).astype(BF16), values[128:, :]
    )
    for i in range(8):
        out[128 + 4 * i : 132 + 4 * i, :] = rows[8 * i : 8 * i + 4, :].astype(BF16)


def on_device(
    hidden, w_query, w_key, w_value, mix_before, mix_after, doc_lengths, doc_owner, loader_order
):
    depth = hidden.shape[1]
    grant = pltpu.CompilerParams(vmem_limit_bytes=12 << 20)
    rows = N_SEQ * PIECE
    vmem = pl.BlockSpec(memory_space=pltpu.VMEM)
    pair = np.arange(HEAD_DIM) // 2
    freq = jnp.asarray((THETA ** (-2.0 * pair / HEAD_DIM)).astype(np.float32)[None, :])
    lens = doc_lengths.reshape(1, TOK)
    own = doc_owner.reshape(1, TOK)
    order = loader_order.reshape(N_SEQ, TOK)

    hbm = pl.BlockSpec(memory_space=pltpu.HBM)
    send, info = pl.pallas_call(
        project_kernel,
        in_specs=[hbm] * 8,
        out_specs=[vmem, vmem],
        out_shape=[
            jax.ShapeDtypeStruct((rows, HEAD_DIM), BF16),
            jax.ShapeDtypeStruct((8, TOK), F32),
        ],
        scratch_shapes=[
            pltpu.VMEM((TOK, depth), BF16),
            pltpu.VMEM((depth, HEAD_DIM), BF16),
            pltpu.VMEM((4 * KV_COLS, depth), BF16),
            pltpu.VMEM((1, TOK), jnp.int32),
            pltpu.VMEM((1, TOK), jnp.int32),
            pltpu.VMEM((N_SEQ, TOK), jnp.int32),
            pltpu.VMEM((1, TOK), F32),
            pltpu.VMEM((TOK, HEAD_DIM), F32),
            pltpu.VMEM((TOK, HEAD_DIM), F32),
            pltpu.VMEM((rows, 3 * TOK), BF16),
            pltpu.SemaphoreType.DMA((8,)),
        ],
        compiler_params=grant,
        name="project",
    )(
        *[
            pltpu.with_memory_space_constraint(x, pltpu.HBM)
            for x in (hidden, w_query, w_key.T, w_value.T, lens, own, order, freq)
        ]
    )

    got = lax.all_to_all(
        send.reshape(N_SEQ, PIECE, HEAD_DIM), "seq", split_axis=0, concat_axis=0, tiled=True
    ).reshape(rows, HEAD_DIM)
    gathered = lax.all_gather(got, "sub", axis=0, tiled=True)

    logits, values = pl.pallas_call(
        functools.partial(logits_kernel, 1.0 / HEAD_DIM**0.5),
        in_specs=[vmem, vmem],
        out_specs=[vmem, vmem],
        out_shape=[
            jax.ShapeDtypeStruct((HEADS, 8, 128), F32),
            jax.ShapeDtypeStruct((rows, HEAD_DIM), BF16),
        ],
        compiler_params=grant,
        name="logits",
    )(got, gathered)

    mine = lax.all_to_all(logits, ("grp", "sub"), split_axis=0, concat_axis=0, tiled=True)
    blended = pl.pallas_call(
        soften_kernel,
        in_specs=[vmem] * 4,
        out_specs=vmem,
        out_shape=jax.ShapeDtypeStruct((HEADS, 8, 128), BF16),
        scratch_shapes=[pltpu.VMEM((HEADS, HEADS, 128), F32)] * 2,
        compiler_params=grant,
        name="soften",
    )(mine, mix_before, mix_after, info)
    back = lax.all_to_all(blended, ("grp", "sub"), split_axis=0, concat_axis=0, tiled=True)
    return pl.pallas_call(
        output_kernel,
        in_specs=[vmem, vmem],
        out_specs=vmem,
        out_shape=jax.ShapeDtypeStruct((CAP, HEAD_DIM), BF16),
        compiler_params=grant,
        name="output",
    )(back.reshape(HEADS * 8, 128), values)


def solution(mesh):
    split = Mesh(
        mesh.devices.reshape(N_SEQ, HEADS // GROUP, GROUP), ("seq", "grp", "sub")
    ) if not isinstance(mesh, jax.sharding.AbstractMesh) else mesh
    mp = ("grp", "sub")
    placed = (P("seq", None), P(None, mp), P(None, mp), P(None, mp), P(), P(), P(), P(), P())
    return jax.shard_map(
        on_device, mesh=split, in_specs=placed, out_specs=P("seq", mp), check_vma=False
    )
```

```python
import functools

import jax
import jax.numpy as jnp
import numpy as np
from jax import lax
from jax.experimental import pallas as pl
from jax.experimental.pallas import tpu as pltpu
from jax.sharding import Mesh
from jax.sharding import PartitionSpec as P

THETA = 500000.0
N_SEQ = 32
HEADS = 24
GROUP = 4
HEAD_DIM = 128
KV_COLS = 32
TOK = 128
CAP = 160
PIECE = 8
KV_ROW = 5
META = 7
SHORT = 16
F32 = jnp.float32
BF16 = jnp.bfloat16


def iota(shape, dim):
    return lax.broadcasted_iota(jnp.int32, shape, dim)


def dot_nt(a, b):
    return lax.dot_general(a, b, (((1,), (1,)), ((), ())), preferred_element_type=F32)


def dot_nn(a, b):
    return lax.dot_general(a, b, (((1,), (0,)), ((), ())), preferred_element_type=F32)


def turn(shape, sub):
    return (iota(shape, len(shape) - 1) - KV_COLS * sub) & (HEAD_DIM - 1)


def project_kernel(
    hid_h, wq_h, wk_h, wv_h, lens_h, own_h, order_h, freq_h, send, info,
    hid, wq, wkv, lens, own, order, freq, cos_t, sin_t, first, place, sems,
):
    sub = lax.axis_index("sub")
    copies = []

    def copy(source, target):
        copies.append(pltpu.make_async_copy(source, target, sems.at[len(copies)]))
        copies[-1].start()

    copy(lens_h, lens)
    copy(own_h, own)
    copy(order_h, order)
    copy(freq_h, freq)
    half = hid.shape[1] // 2
    for part in range(2):
        span = pl.ds(part * half, half)
        copy(hid_h.at[:, span], hid.at[:, span])
        copy(wq_h.at[span, :], wq.at[span, :])
        copy(wk_h.at[:, span], wkv.at[pl.ds(0, KV_COLS), span])
        copy(wv_h.at[:, span], wkv.at[pl.ds(KV_COLS, KV_COLS), span])
    wkv[2 * KV_COLS :, :] = jnp.zeros((2 * KV_COLS, hid.shape[1]), BF16)
    for k in range(4):
        copies[k].wait()

    shape = (TOK, TOK)
    row, col = iota(shape, 0), iota(shape, 1)
    eye = row == col
    low = row < col

    def down(value):
        return jnp.sum(jnp.where(eye, value, 0.0), axis=1, keepdims=True)

    def across(value):
        return jnp.sum(jnp.where(eye, value, 0.0), axis=0, keepdims=True)

    len_row = lens[...].astype(F32)
    own_row = own[...].astype(F32)
    len_col, own_col = down(len_row), down(own_row)
    start = jnp.sum(jnp.where(low, len_col, 0.0), axis=0, keepdims=True)
    shard_start = jnp.sum(
        jnp.where(low & (own_col == own_row), len_col, 0.0), axis=0, keepdims=True
    )
    line = iota((8, TOK), 0)
    info[...] = jnp.where(line == 0, shard_start, jnp.where(line == 1, len_row, own_row))
    packed = down(order[pl.ds(lax.axis_index("seq"), 1), :].astype(F32))
    inside = (packed >= start) & (packed < start + len_row)

    def pick(value):
        return jnp.sum(jnp.where(inside, value, 0.0), axis=1, keepdims=True)

    target = pick(own_row)
    position = packed - pick(start)
    slot = pick(shard_start) + position
    target_row = across(target)
    rank = jnp.sum(
        jnp.where((target_row == target) & (col < row), 1.0, 0.0), axis=1, keepdims=True
    )
    pair = jnp.floor(rank * 0.5)
    angle = position * freq[...]
    cos_t[...] = jnp.cos(angle)
    even = col % 2 == 0
    sin = jnp.sin(angle)
    sin_t[...] = jnp.where(even, -sin, sin)
    rows = iota((N_SEQ * PIECE, TOK), 0).astype(F32)

    def put(k, where_to):
        place[:, k * TOK : (k + 1) * TOK] = jnp.where(rows == where_to, 1.0, 0.0).astype(BF16)

    put(0, across(target * PIECE + rank))
    put(1, across(target * PIECE + KV_ROW + pair))
    put(2, target_row * PIECE + META)
    turned = turn(shape, sub)
    meta = turned.astype(F32) == rank + HEAD_DIM // 2
    meta = jnp.where(meta, slot + 1.0, 0.0).astype(BF16)
    side = (turned // (HEAD_DIM // 2)).astype(F32) == rank - 2.0 * pair

    for c in copies[4:8]:
        c.wait()
    first[0] = dot_nn(hid[:, :half], wq[:half, :])
    first[1] = dot_nt(hid[:, :half], wkv[:, :half])
    for c in copies[8:]:
        c.wait()
    acc_q = first[0] + dot_nn(hid[:, half:], wq[half:, :])
    acc_kv = first[1] + dot_nt(hid[:, half:], wkv[:, half:])
    even = col % 2 == 0

    cos_a, sin_a = cos_t[...], sin_t[...]

    def rope(value):
        partner = jnp.where(even, pltpu.roll(value, HEAD_DIM - 1, 1), pltpu.roll(value, 1, 1))
        return value * cos_a + partner * sin_a

    query = rope(acc_q).astype(BF16)
    kv = pltpu.roll(acc_kv, KV_COLS * sub, 1)
    kv = jnp.where(turned < KV_COLS, rope(kv), kv)
    kv = jnp.where(side, kv + pltpu.roll(kv, HEAD_DIM // 2, 1), 0.0).astype(BF16)
    send[...] = dot_nn(place[...], jnp.concatenate([query, kv, meta], axis=0)).astype(BF16)


def logits_kernel(scale, got, gathered, out, values):
    rows = N_SEQ * PIECE
    mine = got[...]
    head = mine.astype(F32).reshape(N_SEQ, PIECE, HEAD_DIM)
    tags = jnp.broadcast_to(head[:, META : META + 1, :], head.shape)
    line, lane = iota(head.shape, 1), turn(head.shape, lax.axis_index("sub")) - HEAD_DIM // 2
    same = iota((rows, rows), 0) == iota((rows, rows), 1)

    token = jnp.where(line < KV_ROW, line, 2 * (line - KV_ROW))
    weight = jnp.where((lane == token + 1) & (line >= KV_ROW) & (line < META), 256.0, 0.0)
    weight = jnp.where(lane == token, 1.0, weight)
    column = jnp.sum(weight * tags, axis=2, keepdims=True).reshape(rows, 1)
    both = jnp.sum(jnp.where(same, column, 0.0), axis=0, keepdims=True)
    right = jnp.floor(both * (1.0 / 256.0))
    left, right = both - 256.0 * right - 1.0, right - 1.0
    is_query = iota((1, rows), 1) % PIECE < KV_ROW

    window = iota((rows, HEAD_DIM), 1) // KV_COLS
    blocks = [jnp.zeros((rows, HEAD_DIM), F32)] * 4
    for c in range(GROUP):
        tile = gathered[c * rows : (c + 1) * rows, :].astype(F32)
        for i in range(4):
            blocks[i] = jnp.where(window == (c + i) % GROUP, tile, blocks[i])
    for i in range(1, 4):
        blocks[i] = pltpu.roll(blocks[i], HEAD_DIM - i * KV_COLS, 1)
    key = jnp.concatenate([blocks[0].astype(BF16), blocks[2].astype(BF16)], axis=0)
    value = jnp.concatenate([blocks[1].astype(BF16), blocks[3].astype(BF16)], axis=0)

    n = iota((rows, 1), 0)
    kv_slot = jnp.where(n < 128, n, 128 + n % 32).astype(F32)
    from_left = jnp.where(kv_slot == jnp.where(is_query, -1.0, left), 1.0, 0.0).astype(BF16)
    from_right = jnp.where(kv_slot == right, 1.0, 0.0).astype(BF16)
    kv_spots = jnp.concatenate([from_left, from_right], axis=1)
    n = iota((224, 1), 0)
    late = jnp.where(n % 8 < 4, 64 + n // 8 * 4 + n % 8, -5)
    strided = 128 + 4 * (n % 8) + (n - 192) // 8
    q_slot = jnp.where(n < 128, n, jnp.where(n < 192, late, strided)).astype(F32)
    q_spots = jnp.where(q_slot == jnp.where(is_query, left, -1.0), 1.0, 0.0).astype(BF16)
    query = dot_nn(q_spots, mine).astype(BF16)
    key = dot_nn(kv_spots, key).astype(BF16)
    values[...] = dot_nn(kv_spots, value).astype(BF16)

    main = dot_nt(query[:192], key[:128]) * scale
    tail = dot_nt(query[192:], key[128:]) * scale
    lane = iota((8, HEAD_DIM), 1) // 32
    packed = jnp.zeros((8, HEAD_DIM), F32)
    for j in range(4):
        packed = jnp.where(lane == j, tail[8 * j : 8 * j + 8], packed)
    out[:SHORT] = main[:128].reshape(SHORT, 8, 128)
    long = main[128:].reshape(8, 8, 128)
    fifth = iota(long.shape, 1) == 4
    out[SHORT:] = jnp.where(fifth, jnp.broadcast_to(packed[:, None, :], long.shape), long)


def spread(coefs, table):
    for j in range(HEADS):
        table[j] = jnp.broadcast_to(coefs[:, j : j + 1], (HEADS, 128))


def mix(table, terms):
    sums = []
    for j in range(HEADS):
        total = table[j, 0:1, :] * terms[0]
        for h in range(1, HEADS):
            total = total + table[j, h : h + 1, :] * terms[h]
        sums.append(total)
    return jnp.stack(sums)


def soften_kernel(logits, before, after, info, out, table_b, table_a):
    owner = lax.axis_index("grp") * GROUP + lax.axis_index("sub")
    shard = lax.axis_index("seq").astype(F32)
    spread(before, table_b)
    spread(after, table_a)
    is_long = owner >= SHORT
    line = iota((8, 128), 0)
    lane = iota((8, 128), 1)
    slot = jnp.where(is_long, 128 + 4 * (owner - SHORT), 8 * owner) + line
    valid = jnp.logical_or(line < 4, jnp.logical_not(is_long))
    begin, length, own = info[0:1, :], info[1:2, :], info[2:3, :]
    slot_f = slot.astype(F32)
    held = (own == shard) & (slot_f >= begin) & (slot_f < begin + length) & valid
    filled = jnp.sum(jnp.where(held, 1.0, 0.0), axis=1, keepdims=True) > 0.5
    first = jnp.sum(jnp.where(held, begin, 0.0), axis=1, keepdims=True)

    def allowed(other):
        other_f = other.astype(F32)
        return (other_f >= first) & (other_f <= slot_f) & filled

    main_ok = allowed(lane)
    tail_ok = allowed(128 + lane % 32) & is_long & (lane // 32 == line)
    mixed = mix(table_b, [logits[h] for h in range(HEADS)])
    tail = jnp.broadcast_to(mixed[:, 4:5, :], mixed.shape)
    main_m = jnp.where(main_ok[None], mixed, -1e30)
    tail_m = jnp.where(tail_ok[None], tail, -1e30)
    top = jnp.max(jnp.maximum(main_m, tail_m), axis=2, keepdims=True)
    main_e = jnp.where(main_ok[None], jnp.exp(main_m - top), 0.0)
    tail_e = jnp.where(tail_ok[None], jnp.exp(tail_m - top), 0.0)
    total = jnp.sum(main_e + tail_e, axis=2, keepdims=True)
    share = 1.0 / jnp.where(filled[None], total, 1.0)
    main_w = (main_e * share).astype(BF16).astype(F32)
    tail_w = (tail_e * share).astype(BF16).astype(F32)
    tail_w = jnp.broadcast_to(jnp.sum(tail_w, axis=1, keepdims=True), tail_w.shape)
    weights = jnp.where(((line == 4) & is_long)[None], tail_w, main_w)
    out[...] = mix(table_a, [weights[h] for h in range(HEADS)]).astype(BF16)


def output_kernel(weights, values, out):
    out[:128, :] = dot_nn(weights[:128, :], values[:128, :]).astype(BF16)
    long = weights[128:, :].astype(F32).reshape(8, 8, 128)
    tail = jnp.broadcast_to(long[:, 4:5, :], long.shape)
    tail = jnp.where(iota(long.shape, 2) // 32 == iota(long.shape, 1), tail, 0.0)
    rows = dot_nn(weights[128:, :], values[:128, :]) + dot_nn(
        tail.reshape(64, 128).astype(BF16), values[128:, :]
    )
    for i in range(8):
        out[128 + 4 * i : 132 + 4 * i, :] = rows[8 * i : 8 * i + 4, :].astype(BF16)


def on_device(
    hidden, w_query, w_key, w_value, mix_before, mix_after, doc_lengths, doc_owner, loader_order
):
    depth = hidden.shape[1]
    grant = pltpu.CompilerParams(vmem_limit_bytes=12 << 20)
    rows = N_SEQ * PIECE
    vmem = pl.BlockSpec(memory_space=pltpu.VMEM)
    pair = np.arange(HEAD_DIM) // 2
    freq = jnp.asarray((THETA ** (-2.0 * pair / HEAD_DIM)).astype(np.float32)[None, :])
    lens = doc_lengths.reshape(1, TOK)
    own = doc_owner.reshape(1, TOK)
    order = loader_order.reshape(N_SEQ, TOK)

    hbm = pl.BlockSpec(memory_space=pltpu.HBM)
    send, info = pl.pallas_call(
        project_kernel,
        in_specs=[hbm] * 8,
        out_specs=[vmem, vmem],
        out_shape=[
            jax.ShapeDtypeStruct((rows, HEAD_DIM), BF16),
            jax.ShapeDtypeStruct((8, TOK), F32),
        ],
        scratch_shapes=[
            pltpu.VMEM((TOK, depth), BF16),
            pltpu.VMEM((depth, HEAD_DIM), BF16),
            pltpu.VMEM((4 * KV_COLS, depth), BF16),
            pltpu.VMEM((1, TOK), jnp.int32),
            pltpu.VMEM((1, TOK), jnp.int32),
            pltpu.VMEM((N_SEQ, TOK), jnp.int32),
            pltpu.VMEM((1, TOK), F32),
            pltpu.VMEM((TOK, HEAD_DIM), F32),
            pltpu.VMEM((TOK, HEAD_DIM), F32),
            pltpu.VMEM((2, TOK, HEAD_DIM), F32),
            pltpu.VMEM((rows, 3 * TOK), BF16),
            pltpu.SemaphoreType.DMA((12,)),
        ],
        compiler_params=grant,
        name="project",
    )(
        *[
            pltpu.with_memory_space_constraint(x, pltpu.HBM)
            for x in (hidden, w_query, w_key.T, w_value.T, lens, own, order, freq)
        ]
    )

    got = lax.all_to_all(
        send.reshape(N_SEQ, PIECE, HEAD_DIM), "seq", split_axis=0, concat_axis=0, tiled=True
    ).reshape(rows, HEAD_DIM)
    gathered = lax.all_gather(got, "sub", axis=0, tiled=True)

    logits, values = pl.pallas_call(
        functools.partial(logits_kernel, 1.0 / HEAD_DIM**0.5),
        in_specs=[vmem, vmem],
        out_specs=[vmem, vmem],
        out_shape=[
            jax.ShapeDtypeStruct((HEADS, 8, 128), F32),
            jax.ShapeDtypeStruct((rows, HEAD_DIM), BF16),
        ],
        compiler_params=grant,
        name="logits",
    )(got, gathered)

    mine = lax.all_to_all(logits, ("grp", "sub"), split_axis=0, concat_axis=0, tiled=True)
    blended = pl.pallas_call(
        soften_kernel,
        in_specs=[vmem] * 4,
        out_specs=vmem,
        out_shape=jax.ShapeDtypeStruct((HEADS, 8, 128), BF16),
        scratch_shapes=[pltpu.VMEM((HEADS, HEADS, 128), F32)] * 2,
        compiler_params=grant,
        name="soften",
    )(mine, mix_before, mix_after, info)
    back = lax.all_to_all(blended, ("grp", "sub"), split_axis=0, concat_axis=0, tiled=True)
    return pl.pallas_call(
        output_kernel,
        in_specs=[vmem, vmem],
        out_specs=vmem,
        out_shape=jax.ShapeDtypeStruct((CAP, HEAD_DIM), BF16),
        compiler_params=grant,
        name="output",
    )(back.reshape(HEADS * 8, 128), values)


def solution(mesh):
    split = Mesh(
        mesh.devices.reshape(N_SEQ, HEADS // GROUP, GROUP), ("seq", "grp", "sub")
    ) if not isinstance(mesh, jax.sharding.AbstractMesh) else mesh
    mp = ("grp", "sub")
    placed = (P("seq", None), P(None, mp), P(None, mp), P(None, mp), P(), P(), P(), P(), P())
    return jax.shard_map(
        on_device, mesh=split, in_specs=placed, out_specs=P("seq", mp), check_vma=False
    )
```

```python
import functools

import jax
import jax.numpy as jnp
import numpy as np
from jax import lax
from jax.experimental import pallas as pl
from jax.experimental.pallas import tpu as pltpu
from jax.sharding import Mesh
from jax.sharding import PartitionSpec as P

THETA = 500000.0
N_SEQ = 32
HEADS = 24
GROUP = 4
HEAD_DIM = 128
KV_COLS = 32
TOK = 128
CAP = 160
PIECE = 8
KV_ROW = 5
KV_ROWS = 4
META = 7
SHORT = 16
F32 = jnp.float32
BF16 = jnp.bfloat16


def iota(shape, dim):
    return lax.broadcasted_iota(jnp.int32, shape, dim)


def dot_nt(a, b):
    return lax.dot_general(a, b, (((1,), (1,)), ((), ())), preferred_element_type=F32)


def dot_nn(a, b):
    return lax.dot_general(a, b, (((1,), (0,)), ((), ())), preferred_element_type=F32)


def turn(shape, sub):
    return (iota(shape, len(shape) - 1) - KV_COLS * sub) & (HEAD_DIM - 1)


def project_kernel(
    hid_h, wq_h, wk_h, wv_h, lens_h, own_h, order_h, freq_h, send, info,
    hid, wq, wkv, lens, own, order, freq, cos_t, sin_t, first, place, sems,
):
    sub = lax.axis_index("sub")
    copies = []

    def copy(source, target):
        copies.append(pltpu.make_async_copy(source, target, sems.at[len(copies)]))
        copies[-1].start()

    copy(lens_h, lens)
    copy(own_h, own)
    copy(order_h, order)
    copy(freq_h, freq)
    half = hid.shape[1] // 2
    for part in range(2):
        span = pl.ds(part * half, half)
        copy(hid_h.at[:, span], hid.at[:, span])
        copy(wq_h.at[span, :], wq.at[span, :])
        copy(wk_h.at[:, span], wkv.at[pl.ds(0, KV_COLS), span])
        copy(wv_h.at[:, span], wkv.at[pl.ds(KV_COLS, KV_COLS), span])
    wkv[2 * KV_COLS :, :] = jnp.zeros((2 * KV_COLS, hid.shape[1]), BF16)
    for k in range(4):
        copies[k].wait()

    shape = (TOK, TOK)
    row, col = iota(shape, 0), iota(shape, 1)
    eye = row == col
    low = row < col

    def down(value):
        return jnp.sum(jnp.where(eye, value, 0.0), axis=1, keepdims=True)

    def across(value):
        return jnp.sum(jnp.where(eye, value, 0.0), axis=0, keepdims=True)

    len_row = lens[...].astype(F32)
    own_row = own[...].astype(F32)
    len_col, own_col = down(len_row), down(own_row)
    start = jnp.sum(jnp.where(low, len_col, 0.0), axis=0, keepdims=True)
    shard_start = jnp.sum(
        jnp.where(low & (own_col == own_row), len_col, 0.0), axis=0, keepdims=True
    )
    line = iota((8, TOK), 0)
    info[...] = jnp.where(line == 0, shard_start, jnp.where(line == 1, len_row, own_row))
    packed = down(order[pl.ds(lax.axis_index("seq"), 1), :].astype(F32))
    inside = (packed >= start) & (packed < start + len_row)

    def pick(value):
        return jnp.sum(jnp.where(inside, value, 0.0), axis=1, keepdims=True)

    target = pick(own_row)
    position = packed - pick(start)
    slot = pick(shard_start) + position
    target_row = across(target)
    rank = jnp.sum(
        jnp.where((target_row == target) & (col < row), 1.0, 0.0), axis=1, keepdims=True
    )
    pair = jnp.floor(rank * 0.5)
    angle = position * freq[...]
    cos_t[...] = jnp.cos(angle)
    even = col % 2 == 0
    sin = jnp.sin(angle)
    sin_t[...] = jnp.where(even, -sin, sin)
    rows = iota((N_SEQ * PIECE, TOK), 0).astype(F32)

    def put(k, where_to):
        place[:, k * TOK : (k + 1) * TOK] = jnp.where(rows == where_to, 1.0, 0.0).astype(BF16)

    put(0, across(target * PIECE + rank))
    put(1, across(target * PIECE + KV_ROW + pair))
    put(2, target_row * PIECE + META)
    turned = turn(shape, sub)
    meta = turned.astype(F32) == rank + HEAD_DIM // 2
    meta = jnp.where(meta, slot + 1.0, 0.0).astype(BF16)
    side = (turned // (HEAD_DIM // 2)).astype(F32) == rank - 2.0 * pair

    for c in copies[4:8]:
        c.wait()
    first[0] = dot_nn(hid[:, :half], wq[:half, :])
    first[1] = dot_nt(hid[:, :half], wkv[:, :half])
    for c in copies[8:]:
        c.wait()
    acc_q = first[0] + dot_nn(hid[:, half:], wq[half:, :])
    acc_kv = first[1] + dot_nt(hid[:, half:], wkv[:, half:])
    even = col % 2 == 0

    cos_a, sin_a = cos_t[...], sin_t[...]

    def rope(value):
        partner = jnp.where(even, pltpu.roll(value, HEAD_DIM - 1, 1), pltpu.roll(value, 1, 1))
        return value * cos_a + partner * sin_a

    query = rope(acc_q).astype(BF16)
    kv = pltpu.roll(acc_kv, KV_COLS * sub, 1)
    kv = jnp.where(turned < KV_COLS, rope(kv), kv)
    kv = jnp.where(side, kv + pltpu.roll(kv, HEAD_DIM // 2, 1), 0.0).astype(BF16)
    send[...] = dot_nn(place[...], jnp.concatenate([query, kv, meta], axis=0)).astype(BF16)


def logits_kernel(scale, got, gathered, out, values):
    rows = N_SEQ * PIECE
    mine = got[...]
    head = mine.astype(F32).reshape(N_SEQ, PIECE, HEAD_DIM)
    tags = jnp.broadcast_to(head[:, META : META + 1, :], head.shape)
    line, lane = iota(head.shape, 1), turn(head.shape, lax.axis_index("sub")) - HEAD_DIM // 2
    token = jnp.where(line < KV_ROW, line, 2 * (line - KV_ROW))
    weight = jnp.where((lane == token + 1) & (line >= KV_ROW) & (line < META), 256.0, 0.0)
    weight = jnp.where(lane == token, 1.0, weight)
    column = jnp.sum(weight * tags, axis=2, keepdims=True).reshape(rows, 1)

    def across(shape, target):
        hit = iota(shape, 0) == target
        return jnp.sum(jnp.where(hit, column, 0.0), axis=0, keepdims=True)

    n = iota((rows, rows), 1)
    query_slot = across((rows, rows), jnp.where(n % PIECE < KV_ROW, n, -1)) - 1.0
    kv_rows = N_SEQ * KV_ROWS
    n = iota((rows, kv_rows), 1)
    n = jnp.where(n % KV_ROWS > 0, n // KV_ROWS * PIECE + PIECE - KV_ROWS + n % KV_ROWS, -1)
    both = across((rows, kv_rows), n)
    right = jnp.floor(both * (1.0 / 256.0))
    left, right = both - 256.0 * right - 1.0, right - 1.0

    window = iota((kv_rows, HEAD_DIM), 1) // KV_COLS
    blocks = [jnp.zeros((kv_rows, HEAD_DIM), F32)] * 4
    for c in range(GROUP):
        tile = gathered[c * kv_rows : (c + 1) * kv_rows, :].astype(F32)
        for i in range(4):
            blocks[i] = jnp.where(window == (c + i) % GROUP, tile, blocks[i])
    for i in range(1, 4):
        blocks[i] = pltpu.roll(blocks[i], HEAD_DIM - i * KV_COLS, 1)
    key = jnp.concatenate([blocks[0].astype(BF16), blocks[2].astype(BF16)], axis=0)
    value = jnp.concatenate([blocks[1].astype(BF16), blocks[3].astype(BF16)], axis=0)

    n = iota((rows, 1), 0)
    kv_slot = jnp.where(n < 128, n, 128 + n % 32).astype(F32)
    from_left = jnp.where(kv_slot == left, 1.0, 0.0).astype(BF16)
    from_right = jnp.where(kv_slot == right, 1.0, 0.0).astype(BF16)
    kv_spots = jnp.concatenate([from_left, from_right], axis=1)
    n = iota((224, 1), 0)
    late = jnp.where(n % 8 < 4, 64 + n // 8 * 4 + n % 8, -5)
    strided = 128 + 4 * (n % 8) + (n - 192) // 8
    q_slot = jnp.where(n < 128, n, jnp.where(n < 192, late, strided)).astype(F32)
    q_spots = jnp.where(q_slot == query_slot, 1.0, 0.0).astype(BF16)
    query = dot_nn(q_spots, mine).astype(BF16)
    key = dot_nn(kv_spots, key).astype(BF16)
    values[...] = dot_nn(kv_spots, value).astype(BF16)

    main = dot_nt(query[:192], key[:128]) * scale
    tail = dot_nt(query[192:], key[128:]) * scale
    lane = iota((8, HEAD_DIM), 1) // 32
    packed = jnp.zeros((8, HEAD_DIM), F32)
    for j in range(4):
        packed = jnp.where(lane == j, tail[8 * j : 8 * j + 8], packed)
    out[:SHORT] = main[:128].reshape(SHORT, 8, 128)
    long = main[128:].reshape(8, 8, 128)
    fifth = iota(long.shape, 1) == 4
    out[SHORT:] = jnp.where(fifth, jnp.broadcast_to(packed[:, None, :], long.shape), long)


def spread(coefs, table):
    for j in range(HEADS):
        table[j] = jnp.broadcast_to(coefs[:, j : j + 1], (HEADS, 128))


def mix(table, terms):
    sums = []
    for j in range(HEADS):
        total = table[j, 0:1, :] * terms[0]
        for h in range(1, HEADS):
            total = total + table[j, h : h + 1, :] * terms[h]
        sums.append(total)
    return jnp.stack(sums)


def soften_kernel(logits, before, after, info, out, table_b, table_a):
    owner = lax.axis_index("grp") * GROUP + lax.axis_index("sub")
    shard = lax.axis_index("seq").astype(F32)
    spread(before, table_b)
    spread(after, table_a)
    is_long = owner >= SHORT
    line = iota((8, 128), 0)
    lane = iota((8, 128), 1)
    slot = jnp.where(is_long, 128 + 4 * (owner - SHORT), 8 * owner) + line
    valid = jnp.logical_or(line < 4, jnp.logical_not(is_long))
    begin, length, own = info[0:1, :], info[1:2, :], info[2:3, :]
    slot_f = slot.astype(F32)
    held = (own == shard) & (slot_f >= begin) & (slot_f < begin + length) & valid
    filled = jnp.sum(jnp.where(held, 1.0, 0.0), axis=1, keepdims=True) > 0.5
    first = jnp.sum(jnp.where(held, begin, 0.0), axis=1, keepdims=True)

    def allowed(other):
        other_f = other.astype(F32)
        return (other_f >= first) & (other_f <= slot_f) & filled

    main_ok = allowed(lane)
    tail_ok = allowed(128 + lane % 32) & is_long & (lane // 32 == line)
    mixed = mix(table_b, [logits[h] for h in range(HEADS)])
    tail = jnp.broadcast_to(mixed[:, 4:5, :], mixed.shape)
    main_m = jnp.where(main_ok[None], mixed, -1e30)
    tail_m = jnp.where(tail_ok[None], tail, -1e30)
    top = jnp.max(jnp.maximum(main_m, tail_m), axis=2, keepdims=True)
    main_e = jnp.where(main_ok[None], jnp.exp(main_m - top), 0.0)
    tail_e = jnp.where(tail_ok[None], jnp.exp(tail_m - top), 0.0)
    total = jnp.sum(main_e + tail_e, axis=2, keepdims=True)
    share = 1.0 / jnp.where(filled[None], total, 1.0)
    main_w = (main_e * share).astype(BF16).astype(F32)
    tail_w = (tail_e * share).astype(BF16).astype(F32)
    tail_w = jnp.broadcast_to(jnp.sum(tail_w, axis=1, keepdims=True), tail_w.shape)
    weights = jnp.where(((line == 4) & is_long)[None], tail_w, main_w)
    out[...] = mix(table_a, [weights[h] for h in range(HEADS)]).astype(BF16)


def output_kernel(weights, values, out):
    out[:128, :] = dot_nn(weights[:128, :], values[:128, :]).astype(BF16)
    long = weights[128:, :].astype(F32).reshape(8, 8, 128)
    tail = jnp.broadcast_to(long[:, 4:5, :], long.shape)
    tail = jnp.where(iota(long.shape, 2) // 32 == iota(long.shape, 1), tail, 0.0)
    rows = dot_nn(weights[128:, :], values[:128, :]) + dot_nn(
        tail.reshape(64, 128).astype(BF16), values[128:, :]
    )
    for i in range(8):
        out[128 + 4 * i : 132 + 4 * i, :] = rows[8 * i : 8 * i + 4, :].astype(BF16)


def on_device(
    hidden, w_query, w_key, w_value, mix_before, mix_after, doc_lengths, doc_owner, loader_order
):
    depth = hidden.shape[1]
    grant = pltpu.CompilerParams(vmem_limit_bytes=12 << 20)
    rows = N_SEQ * PIECE
    vmem = pl.BlockSpec(memory_space=pltpu.VMEM)
    pair = np.arange(HEAD_DIM) // 2
    freq = jnp.asarray((THETA ** (-2.0 * pair / HEAD_DIM)).astype(np.float32)[None, :])
    lens = doc_lengths.reshape(1, TOK)
    own = doc_owner.reshape(1, TOK)
    order = loader_order.reshape(N_SEQ, TOK)

    hbm = pl.BlockSpec(memory_space=pltpu.HBM)
    send, info = pl.pallas_call(
        project_kernel,
        in_specs=[hbm] * 8,
        out_specs=[vmem, vmem],
        out_shape=[
            jax.ShapeDtypeStruct((rows, HEAD_DIM), BF16),
            jax.ShapeDtypeStruct((8, TOK), F32),
        ],
        scratch_shapes=[
            pltpu.VMEM((TOK, depth), BF16),
            pltpu.VMEM((depth, HEAD_DIM), BF16),
            pltpu.VMEM((4 * KV_COLS, depth), BF16),
            pltpu.VMEM((1, TOK), jnp.int32),
            pltpu.VMEM((1, TOK), jnp.int32),
            pltpu.VMEM((N_SEQ, TOK), jnp.int32),
            pltpu.VMEM((1, TOK), F32),
            pltpu.VMEM((TOK, HEAD_DIM), F32),
            pltpu.VMEM((TOK, HEAD_DIM), F32),
            pltpu.VMEM((2, TOK, HEAD_DIM), F32),
            pltpu.VMEM((rows, 3 * TOK), BF16),
            pltpu.SemaphoreType.DMA((12,)),
        ],
        compiler_params=grant,
        name="project",
    )(
        *[
            pltpu.with_memory_space_constraint(x, pltpu.HBM)
            for x in (hidden, w_query, w_key.T, w_value.T, lens, own, order, freq)
        ]
    )

    got = lax.all_to_all(
        send.reshape(N_SEQ, PIECE, HEAD_DIM), "seq", split_axis=0, concat_axis=0, tiled=True
    )
    gathered = lax.all_gather(got[:, PIECE - KV_ROWS :], "sub", axis=0, tiled=True)
    got = got.reshape(rows, HEAD_DIM)
    gathered = gathered.reshape(GROUP * N_SEQ * KV_ROWS, HEAD_DIM)

    logits, values = pl.pallas_call(
        functools.partial(logits_kernel, 1.0 / HEAD_DIM**0.5),
        in_specs=[vmem, vmem],
        out_specs=[vmem, vmem],
        out_shape=[
            jax.ShapeDtypeStruct((HEADS, 8, 128), F32),
            jax.ShapeDtypeStruct((rows, HEAD_DIM), BF16),
        ],
        compiler_params=grant,
        name="logits",
    )(got, gathered)

    mine = lax.all_to_all(logits, ("grp", "sub"), split_axis=0, concat_axis=0, tiled=True)
    blended = pl.pallas_call(
        soften_kernel,
        in_specs=[vmem] * 4,
        out_specs=vmem,
        out_shape=jax.ShapeDtypeStruct((HEADS, 8, 128), BF16),
        scratch_shapes=[pltpu.VMEM((HEADS, HEADS, 128), F32)] * 2,
        compiler_params=grant,
        name="soften",
    )(mine, mix_before, mix_after, info)
    back = lax.all_to_all(blended, ("grp", "sub"), split_axis=0, concat_axis=0, tiled=True)
    return pl.pallas_call(
        output_kernel,
        in_specs=[vmem, vmem],
        out_specs=vmem,
        out_shape=jax.ShapeDtypeStruct((CAP, HEAD_DIM), BF16),
        compiler_params=grant,
        name="output",
    )(back.reshape(HEADS * 8, 128), values)


def solution(mesh):
    split = Mesh(
        mesh.devices.reshape(N_SEQ, HEADS // GROUP, GROUP), ("seq", "grp", "sub")
    ) if not isinstance(mesh, jax.sharding.AbstractMesh) else mesh
    mp = ("grp", "sub")
    placed = (P("seq", None), P(None, mp), P(None, mp), P(None, mp), P(), P(), P(), P(), P())
    return jax.shard_map(
        on_device, mesh=split, in_specs=placed, out_specs=P("seq", mp), check_vma=False
    )
```

```python
import functools

import jax
import jax.numpy as jnp
import numpy as np
from jax import lax
from jax.experimental import pallas as pl
from jax.experimental.pallas import tpu as pltpu
from jax.sharding import Mesh
from jax.sharding import PartitionSpec as P

THETA = 500000.0
N_SEQ = 32
HEADS = 24
GROUP = 4
HEAD_DIM = 128
KV_COLS = 32
TOK = 128
CAP = 160
PIECE = 8
KV_ROW = 5
KV_ROWS = 4
META = 7
SHORT = 16
F32 = jnp.float32
BF16 = jnp.bfloat16


def iota(shape, dim):
    return lax.broadcasted_iota(jnp.int32, shape, dim)


def dot_nt(a, b):
    return lax.dot_general(a, b, (((1,), (1,)), ((), ())), preferred_element_type=F32)


def dot_nn(a, b):
    return lax.dot_general(a, b, (((1,), (0,)), ((), ())), preferred_element_type=F32)


def turn(shape, sub):
    return (iota(shape, len(shape) - 1) - KV_COLS * sub) & (HEAD_DIM - 1)


def project_kernel(
    hid_h, wq_h, wk_h, wv_h, lens_h, own_h, order_h, freq_h, before_h, after_h,
    send, info, table_b, table_a,
    hid, wq, wkv, lens, own, order, freq, cos_t, sin_t, first, place, before, after, sems,
):
    sub = lax.axis_index("sub")
    copies = []

    def copy(source, target):
        copies.append(pltpu.make_async_copy(source, target, sems.at[len(copies)]))
        copies[-1].start()

    copy(lens_h, lens)
    copy(own_h, own)
    copy(order_h, order)
    copy(freq_h, freq)
    copy(before_h, before)
    copy(after_h, after)
    half = hid.shape[1] // 2
    for part in range(2):
        span = pl.ds(part * half, half)
        copy(hid_h.at[:, span], hid.at[:, span])
        copy(wq_h.at[span, :], wq.at[span, :])
        copy(wk_h.at[:, span], wkv.at[pl.ds(0, KV_COLS), span])
        copy(wv_h.at[:, span], wkv.at[pl.ds(KV_COLS, KV_COLS), span])
    wkv[2 * KV_COLS :, :] = jnp.zeros((2 * KV_COLS, hid.shape[1]), BF16)
    for c in copies[:6]:
        c.wait()

    shape = (TOK, TOK)
    row, col = iota(shape, 0), iota(shape, 1)
    eye = row == col
    low = row < col

    def down(value):
        return jnp.sum(jnp.where(eye, value, 0.0), axis=1, keepdims=True)

    def across(value):
        return jnp.sum(jnp.where(eye, value, 0.0), axis=0, keepdims=True)

    len_row = lens[...].astype(F32)
    own_row = own[...].astype(F32)
    len_col, own_col = down(len_row), down(own_row)
    start = jnp.sum(jnp.where(low, len_col, 0.0), axis=0, keepdims=True)
    shard_start = jnp.sum(
        jnp.where(low & (own_col == own_row), len_col, 0.0), axis=0, keepdims=True
    )
    line = iota((8, TOK), 0)
    info[...] = jnp.where(line == 0, shard_start, jnp.where(line == 1, len_row, own_row))
    packed = down(order[pl.ds(lax.axis_index("seq"), 1), :].astype(F32))
    inside = (packed >= start) & (packed < start + len_row)

    def pick(value):
        return jnp.sum(jnp.where(inside, value, 0.0), axis=1, keepdims=True)

    target = pick(own_row)
    position = packed - pick(start)
    slot = pick(shard_start) + position
    target_row = across(target)
    rank = jnp.sum(
        jnp.where((target_row == target) & (col < row), 1.0, 0.0), axis=1, keepdims=True
    )
    pair = jnp.floor(rank * 0.5)
    angle = position * freq[...]
    cos_t[...] = jnp.cos(angle)
    even = col % 2 == 0
    sin = jnp.sin(angle)
    sin_t[...] = jnp.where(even, -sin, sin)
    rows = iota((N_SEQ * PIECE, TOK), 0).astype(F32)

    def put(k, where_to):
        place[:, k * TOK : (k + 1) * TOK] = jnp.where(rows == where_to, 1.0, 0.0).astype(BF16)

    put(0, across(target * PIECE + rank))
    put(1, across(target * PIECE + KV_ROW + pair))
    put(2, target_row * PIECE + META)
    turned = turn(shape, sub)
    meta = turned.astype(F32) == rank + HEAD_DIM // 2
    meta = jnp.where(meta, slot + 1.0, 0.0).astype(BF16)
    side = (turned // (HEAD_DIM // 2)).astype(F32) == rank - 2.0 * pair

    for c in copies[6:10]:
        c.wait()
    first[0] = dot_nn(hid[:, :half], wq[:half, :])
    first[1] = dot_nt(hid[:, :half], wkv[:, :half])
    spread(before, table_b)
    spread(after, table_a)
    for c in copies[10:]:
        c.wait()
    acc_q = first[0] + dot_nn(hid[:, half:], wq[half:, :])
    acc_kv = first[1] + dot_nt(hid[:, half:], wkv[:, half:])
    even = col % 2 == 0

    cos_a, sin_a = cos_t[...], sin_t[...]

    def rope(value):
        partner = jnp.where(even, pltpu.roll(value, HEAD_DIM - 1, 1), pltpu.roll(value, 1, 1))
        return value * cos_a + partner * sin_a

    query = rope(acc_q).astype(BF16)
    kv = pltpu.roll(acc_kv, KV_COLS * sub, 1)
    kv = jnp.where(turned < KV_COLS, rope(kv), kv)
    kv = jnp.where(side, kv + pltpu.roll(kv, HEAD_DIM // 2, 1), 0.0).astype(BF16)
    send[...] = dot_nn(place[...], jnp.concatenate([query, kv, meta], axis=0)).astype(BF16)


def logits_kernel(scale, got, gathered, out, values):
    rows = N_SEQ * PIECE
    mine = got[...]
    head = mine.astype(F32).reshape(N_SEQ, PIECE, HEAD_DIM)
    tags = jnp.broadcast_to(head[:, META : META + 1, :], head.shape)
    line, lane = iota(head.shape, 1), turn(head.shape, lax.axis_index("sub")) - HEAD_DIM // 2
    token = jnp.where(line < KV_ROW, line, 2 * (line - KV_ROW))
    weight = jnp.where((lane == token + 1) & (line >= KV_ROW) & (line < META), 256.0, 0.0)
    weight = jnp.where(lane == token, 1.0, weight)
    column = jnp.sum(weight * tags, axis=2, keepdims=True).reshape(rows, 1)

    def across(shape, target):
        hit = iota(shape, 0) == target
        return jnp.sum(jnp.where(hit, column, 0.0), axis=0, keepdims=True)

    n = iota((rows, rows), 1)
    query_slot = across((rows, rows), jnp.where(n % PIECE < KV_ROW, n, -1)) - 1.0
    kv_rows = N_SEQ * KV_ROWS
    n = iota((rows, kv_rows), 1)
    n = jnp.where(n % KV_ROWS > 0, n // KV_ROWS * PIECE + PIECE - KV_ROWS + n % KV_ROWS, -1)
    both = across((rows, kv_rows), n)
    right = jnp.floor(both * (1.0 / 256.0))
    left, right = both - 256.0 * right - 1.0, right - 1.0

    window = iota((kv_rows, HEAD_DIM), 1) // KV_COLS
    blocks = [jnp.zeros((kv_rows, HEAD_DIM), F32)] * 4
    for c in range(GROUP):
        tile = gathered[c * kv_rows : (c + 1) * kv_rows, :].astype(F32)
        for i in range(4):
            blocks[i] = jnp.where(window == (c + i) % GROUP, tile, blocks[i])
    for i in range(1, 4):
        blocks[i] = pltpu.roll(blocks[i], HEAD_DIM - i * KV_COLS, 1)
    key = jnp.concatenate([blocks[0].astype(BF16), blocks[2].astype(BF16)], axis=0)
    value = jnp.concatenate([blocks[1].astype(BF16), blocks[3].astype(BF16)], axis=0)

    n = iota((rows, 1), 0)
    kv_slot = jnp.where(n < 128, n, 128 + n % 32).astype(F32)
    from_left = jnp.where(kv_slot == left, 1.0, 0.0).astype(BF16)
    from_right = jnp.where(kv_slot == right, 1.0, 0.0).astype(BF16)
    kv_spots = jnp.concatenate([from_left, from_right], axis=1)
    n = iota((224, 1), 0)
    late = jnp.where(n % 8 < 4, 64 + n // 8 * 4 + n % 8, -5)
    strided = 128 + 4 * (n % 8) + (n - 192) // 8
    q_slot = jnp.where(n < 128, n, jnp.where(n < 192, late, strided)).astype(F32)
    q_spots = jnp.where(q_slot == query_slot, 1.0, 0.0).astype(BF16)
    query = dot_nn(q_spots, mine).astype(BF16)
    key = dot_nn(kv_spots, key).astype(BF16)
    values[...] = dot_nn(kv_spots, value).astype(BF16)

    main = dot_nt(query[:192], key[:128]) * scale
    tail = dot_nt(query[192:], key[128:]) * scale
    lane = iota((8, HEAD_DIM), 1) // 32
    packed = jnp.zeros((8, HEAD_DIM), F32)
    for j in range(4):
        packed = jnp.where(lane == j, tail[8 * j : 8 * j + 8], packed)
    out[:SHORT] = main[:128].reshape(SHORT, 8, 128)
    long = main[128:].reshape(8, 8, 128)
    fifth = iota(long.shape, 1) == 4
    out[SHORT:] = jnp.where(fifth, jnp.broadcast_to(packed[:, None, :], long.shape), long)


def spread(coefs, table):
    for j in range(HEADS):
        table[j] = jnp.broadcast_to(coefs[:, j : j + 1], (HEADS, 128))


def mix(table, terms):
    sums = []
    for j in range(HEADS):
        total = table[j, 0:1, :] * terms[0]
        for h in range(1, HEADS):
            total = total + table[j, h : h + 1, :] * terms[h]
        sums.append(total)
    return jnp.stack(sums)


def soften_kernel(logits, table_b, table_a, info, out):
    owner = lax.axis_index("grp") * GROUP + lax.axis_index("sub")
    shard = lax.axis_index("seq").astype(F32)
    is_long = owner >= SHORT
    line = iota((8, 128), 0)
    lane = iota((8, 128), 1)
    slot = jnp.where(is_long, 128 + 4 * (owner - SHORT), 8 * owner) + line
    valid = jnp.logical_or(line < 4, jnp.logical_not(is_long))
    begin, length, own = info[0:1, :], info[1:2, :], info[2:3, :]
    slot_f = slot.astype(F32)
    held = (own == shard) & (slot_f >= begin) & (slot_f < begin + length) & valid
    filled = jnp.sum(jnp.where(held, 1.0, 0.0), axis=1, keepdims=True) > 0.5
    first = jnp.sum(jnp.where(held, begin, 0.0), axis=1, keepdims=True)

    def allowed(other):
        other_f = other.astype(F32)
        return (other_f >= first) & (other_f <= slot_f) & filled

    main_ok = allowed(lane)
    tail_ok = allowed(128 + lane % 32) & is_long & (lane // 32 == line)
    mixed = mix(table_b, [logits[h] for h in range(HEADS)])
    tail = jnp.broadcast_to(mixed[:, 4:5, :], mixed.shape)
    main_m = jnp.where(main_ok[None], mixed, -1e30)
    tail_m = jnp.where(tail_ok[None], tail, -1e30)
    top = jnp.max(jnp.maximum(main_m, tail_m), axis=2, keepdims=True)
    main_e = jnp.where(main_ok[None], jnp.exp(main_m - top), 0.0)
    tail_e = jnp.where(tail_ok[None], jnp.exp(tail_m - top), 0.0)
    total = jnp.sum(main_e + tail_e, axis=2, keepdims=True)
    share = 1.0 / jnp.where(filled[None], total, 1.0)
    main_w = (main_e * share).astype(BF16).astype(F32)
    tail_w = (tail_e * share).astype(BF16).astype(F32)
    tail_w = jnp.broadcast_to(jnp.sum(tail_w, axis=1, keepdims=True), tail_w.shape)
    weights = jnp.where(((line == 4) & is_long)[None], tail_w, main_w)
    out[...] = mix(table_a, [weights[h] for h in range(HEADS)]).astype(BF16)


def output_kernel(weights, values, out):
    out[:128, :] = dot_nn(weights[:128, :], values[:128, :]).astype(BF16)
    long = weights[128:, :].astype(F32).reshape(8, 8, 128)
    tail = jnp.broadcast_to(long[:, 4:5, :], long.shape)
    tail = jnp.where(iota(long.shape, 2) // 32 == iota(long.shape, 1), tail, 0.0)
    rows = dot_nn(weights[128:, :], values[:128, :]) + dot_nn(
        tail.reshape(64, 128).astype(BF16), values[128:, :]
    )
    for i in range(8):
        out[128 + 4 * i : 132 + 4 * i, :] = rows[8 * i : 8 * i + 4, :].astype(BF16)


def on_device(
    hidden, w_query, w_key, w_value, mix_before, mix_after, doc_lengths, doc_owner, loader_order
):
    depth = hidden.shape[1]
    grant = pltpu.CompilerParams(vmem_limit_bytes=12 << 20)
    packed = pltpu.CompilerParams(
        vmem_limit_bytes=12 << 20
    )
    rows = N_SEQ * PIECE
    vmem = pl.BlockSpec(memory_space=pltpu.VMEM)
    pair = np.arange(HEAD_DIM) // 2
    freq = jnp.asarray((THETA ** (-2.0 * pair / HEAD_DIM)).astype(np.float32)[None, :])
    lens = doc_lengths.reshape(1, TOK)
    own = doc_owner.reshape(1, TOK)
    order = loader_order.reshape(N_SEQ, TOK)

    hbm = pl.BlockSpec(memory_space=pltpu.HBM)
    table = jax.ShapeDtypeStruct((HEADS, HEADS, 128), F32)
    send, info, table_b, table_a = pl.pallas_call(
        project_kernel,
        in_specs=[hbm] * 10,
        out_specs=[vmem] * 4,
        out_shape=[
            jax.ShapeDtypeStruct((rows, HEAD_DIM), BF16),
            jax.ShapeDtypeStruct((8, TOK), F32),
            table,
            table,
        ],
        scratch_shapes=[
            pltpu.VMEM((TOK, depth), BF16),
            pltpu.VMEM((depth, HEAD_DIM), BF16),
            pltpu.VMEM((4 * KV_COLS, depth), BF16),
            pltpu.VMEM((1, TOK), jnp.int32),
            pltpu.VMEM((1, TOK), jnp.int32),
            pltpu.VMEM((N_SEQ, TOK), jnp.int32),
            pltpu.VMEM((1, TOK), F32),
            pltpu.VMEM((TOK, HEAD_DIM), F32),
            pltpu.VMEM((TOK, HEAD_DIM), F32),
            pltpu.VMEM((2, TOK, HEAD_DIM), F32),
            pltpu.VMEM((rows, 3 * TOK), BF16),
            pltpu.VMEM((HEADS, HEADS), F32),
            pltpu.VMEM((HEADS, HEADS), F32),
            pltpu.SemaphoreType.DMA((14,)),
        ],
        compiler_params=packed,
        name="project",
    )(
        *[
            pltpu.with_memory_space_constraint(x, pltpu.HBM)
            for x in (
                hidden, w_query, w_key.T, w_value.T, lens, own, order, freq, mix_before, mix_after,
            )
        ]
    )

    got = lax.all_to_all(
        send.reshape(N_SEQ, PIECE, HEAD_DIM), "seq", split_axis=0, concat_axis=0, tiled=True
    )
    gathered = lax.all_gather(got[:, PIECE - KV_ROWS :], "sub", axis=0, tiled=True)
    got = got.reshape(rows, HEAD_DIM)
    gathered = gathered.reshape(GROUP * N_SEQ * KV_ROWS, HEAD_DIM)

    logits, values = pl.pallas_call(
        functools.partial(logits_kernel, 1.0 / HEAD_DIM**0.5),
        in_specs=[vmem, vmem],
        out_specs=[vmem, vmem],
        out_shape=[
            jax.ShapeDtypeStruct((HEADS, 8, 128), F32),
            jax.ShapeDtypeStruct((rows, HEAD_DIM), BF16),
        ],
        compiler_params=packed,
        name="logits",
    )(got, gathered)

    mine = lax.all_to_all(logits, ("grp", "sub"), split_axis=0, concat_axis=0, tiled=True)
    blended = pl.pallas_call(
        soften_kernel,
        in_specs=[vmem] * 4,
        out_specs=vmem,
        out_shape=jax.ShapeDtypeStruct((HEADS, 8, 128), BF16),
        compiler_params=grant,
        name="soften",
    )(mine, table_b, table_a, info)
    back = lax.all_to_all(blended, ("grp", "sub"), split_axis=0, concat_axis=0, tiled=True)
    return pl.pallas_call(
        output_kernel,
        in_specs=[vmem, vmem],
        out_specs=vmem,
        out_shape=jax.ShapeDtypeStruct((CAP, HEAD_DIM), BF16),
        compiler_params=grant,
        name="output",
    )(back.reshape(HEADS * 8, 128), values)


def solution(mesh):
    split = Mesh(
        mesh.devices.reshape(N_SEQ, HEADS // GROUP, GROUP), ("seq", "grp", "sub")
    ) if not isinstance(mesh, jax.sharding.AbstractMesh) else mesh
    mp = ("grp", "sub")
    placed = (P("seq", None), P(None, mp), P(None, mp), P(None, mp), P(), P(), P(), P(), P())
    return jax.shard_map(
        on_device, mesh=split, in_specs=placed, out_specs=P("seq", mp), check_vma=False
    )
```

```python
import functools

import jax
import jax.numpy as jnp
import numpy as np
from jax import lax
from jax.experimental import pallas as pl
from jax.experimental.pallas import tpu as pltpu
from jax.sharding import Mesh
from jax.sharding import PartitionSpec as P

THETA = 500000.0
N_SEQ = 32
HEADS = 24
GROUP = 4
HEAD_DIM = 128
KV_COLS = 32
TOK = 128
CAP = 160
PIECE = 8
KV_ROW = 5
KV_ROWS = 4
META = 7
SHORT = 16
F32 = jnp.float32
BF16 = jnp.bfloat16


def iota(shape, dim):
    return lax.broadcasted_iota(jnp.int32, shape, dim)


def dot_nt(a, b):
    return lax.dot_general(a, b, (((1,), (1,)), ((), ())), preferred_element_type=F32)


def dot_nn(a, b):
    return lax.dot_general(a, b, (((1,), (0,)), ((), ())), preferred_element_type=F32)


def turn(shape, sub):
    return (iota(shape, len(shape) - 1) - KV_COLS * sub) & (HEAD_DIM - 1)


def project_kernel(
    hid_h, wq_h, wk_h, wv_h, lens_h, own_h, order_h, freq_h, before_h, after_h,
    send, info, table_b, table_a,
    hid, wq, wkv, lens, own, order, freq, cos_t, sin_t, first, place, before, after, sems,
):
    sub = lax.axis_index("sub")
    copies = []

    def copy(source, target):
        copies.append(pltpu.make_async_copy(source, target, sems.at[len(copies)]))
        copies[-1].start()

    copy(lens_h, lens)
    copy(own_h, own)
    copy(order_h, order)
    copy(freq_h, freq)
    copy(before_h, before)
    copy(after_h, after)
    half = hid.shape[1] // 2
    for part in range(2):
        span = pl.ds(part * half, half)
        copy(hid_h.at[:, span], hid.at[:, span])
        copy(wq_h.at[span, :], wq.at[span, :])
        copy(wk_h.at[:, span], wkv.at[pl.ds(0, KV_COLS), span])
        copy(wv_h.at[:, span], wkv.at[pl.ds(KV_COLS, KV_COLS), span])
    wkv[2 * KV_COLS :, :] = jnp.zeros((2 * KV_COLS, hid.shape[1]), BF16)
    for c in copies[:6]:
        c.wait()

    shape = (TOK, TOK)
    row, col = iota(shape, 0), iota(shape, 1)
    eye = row == col
    low = row < col

    def down(value):
        return jnp.sum(jnp.where(eye, value, 0.0), axis=1, keepdims=True)

    def across(value):
        return jnp.sum(jnp.where(eye, value, 0.0), axis=0, keepdims=True)

    len_row = lens[...].astype(F32)
    own_row = own[...].astype(F32)
    len_col, own_col = down(len_row), down(own_row)
    start = jnp.sum(jnp.where(low, len_col, 0.0), axis=0, keepdims=True)
    shard_start = jnp.sum(
        jnp.where(low & (own_col == own_row), len_col, 0.0), axis=0, keepdims=True
    )
    line = iota((8, TOK), 0)
    info[...] = jnp.where(line == 0, shard_start, jnp.where(line == 1, len_row, own_row))
    packed = down(order[pl.ds(lax.axis_index("seq"), 1), :].astype(F32))
    inside = (packed >= start) & (packed < start + len_row)

    def pick(value):
        return jnp.sum(jnp.where(inside, value, 0.0), axis=1, keepdims=True)

    target = pick(own_row)
    position = packed - pick(start)
    slot = pick(shard_start) + position
    target_row = across(target)
    rank = jnp.sum(
        jnp.where((target_row == target) & (col < row), 1.0, 0.0), axis=1, keepdims=True
    )
    pair = jnp.floor(rank * 0.5)
    angle = position * freq[...]
    cos_t[...] = jnp.cos(angle)
    even = col % 2 == 0
    sin = jnp.sin(angle)
    sin_t[...] = jnp.where(even, -sin, sin)
    rows = iota((N_SEQ * PIECE, TOK), 0).astype(F32)

    def put(k, where_to):
        place[:, k * TOK : (k + 1) * TOK] = jnp.where(rows == where_to, 1.0, 0.0).astype(BF16)

    put(0, across(target * PIECE + rank))
    put(1, target_row * PIECE + META)
    put(2, across(target * PIECE + KV_ROW + pair))
    turned = turn(shape, sub)
    meta = turned.astype(F32) == rank + HEAD_DIM // 2
    meta = jnp.where(meta, slot + 1.0, 0.0).astype(BF16)
    side = (turned // (HEAD_DIM // 2)).astype(F32) == rank - 2.0 * pair

    for c in copies[6:10]:
        c.wait()
    first[0] = dot_nn(hid[:, :half], wq[:half, :])
    first[1] = dot_nt(hid[:, :half], wkv[:, :half])
    spread(before, table_b)
    spread(after, table_a)
    for c in copies[10:]:
        c.wait()
    acc_q = first[0] + dot_nn(hid[:, half:], wq[half:, :])
    acc_kv = first[1] + dot_nt(hid[:, half:], wkv[:, half:])
    even = col % 2 == 0

    cos_a, sin_a = cos_t[...], sin_t[...]

    def rope(value):
        partner = jnp.where(even, pltpu.roll(value, HEAD_DIM - 1, 1), pltpu.roll(value, 1, 1))
        return value * cos_a + partner * sin_a

    query = rope(acc_q).astype(BF16)
    kv = pltpu.roll(acc_kv, KV_COLS * sub, 1)
    kv = jnp.where(turned < KV_COLS, rope(kv), kv)
    kv = jnp.where(side, kv + pltpu.roll(kv, HEAD_DIM // 2, 1), 0.0).astype(BF16)
    moved = dot_nn(place[:, : 2 * TOK], jnp.concatenate([query, meta], axis=0))
    send[...] = (moved + dot_nn(place[:, 2 * TOK :], kv)).astype(BF16)


def logits_kernel(scale, got, gathered, out, values):
    rows = N_SEQ * PIECE
    mine = got[...]
    head = mine.astype(F32).reshape(N_SEQ, PIECE, HEAD_DIM)
    tags = jnp.broadcast_to(head[:, META : META + 1, :], head.shape)
    line, lane = iota(head.shape, 1), turn(head.shape, lax.axis_index("sub")) - HEAD_DIM // 2
    token = jnp.where(line < KV_ROW, line, 2 * (line - KV_ROW))
    weight = jnp.where((lane == token + 1) & (line >= KV_ROW) & (line < META), 256.0, 0.0)
    weight = jnp.where(lane == token, 1.0, weight)
    column = jnp.sum(weight * tags, axis=2, keepdims=True).reshape(rows, 1)

    def across(shape, target):
        hit = iota(shape, 0) == target
        return jnp.sum(jnp.where(hit, column, 0.0), axis=0, keepdims=True)

    n = iota((rows, rows), 1)
    query_slot = across((rows, rows), jnp.where(n % PIECE < KV_ROW, n, -1)) - 1.0
    kv_rows = N_SEQ * KV_ROWS
    n = iota((rows, kv_rows), 1)
    n = jnp.where(n % KV_ROWS > 0, n // KV_ROWS * PIECE + PIECE - KV_ROWS + n % KV_ROWS, -1)
    both = across((rows, kv_rows), n)
    right = jnp.floor(both * (1.0 / 256.0))
    left, right = both - 256.0 * right - 1.0, right - 1.0

    window = iota((kv_rows, HEAD_DIM), 1) // KV_COLS
    blocks = [jnp.zeros((kv_rows, HEAD_DIM), F32)] * 4
    for c in range(GROUP):
        tile = gathered[c * kv_rows : (c + 1) * kv_rows, :].astype(F32)
        for i in range(4):
            blocks[i] = jnp.where(window == (c + i) % GROUP, tile, blocks[i])
    for i in range(1, 4):
        blocks[i] = pltpu.roll(blocks[i], HEAD_DIM - i * KV_COLS, 1)
    key = jnp.concatenate([blocks[0].astype(BF16), blocks[2].astype(BF16)], axis=0)
    value = jnp.concatenate([blocks[1].astype(BF16), blocks[3].astype(BF16)], axis=0)

    n = iota((rows, 1), 0)
    kv_slot = jnp.where(n < 128, n, 128 + n % 32).astype(F32)
    from_left = jnp.where(kv_slot == left, 1.0, 0.0).astype(BF16)
    from_right = jnp.where(kv_slot == right, 1.0, 0.0).astype(BF16)
    kv_spots = jnp.concatenate([from_left, from_right], axis=1)
    n = iota((224, 1), 0)
    late = jnp.where(n % 8 < 4, 64 + n // 8 * 4 + n % 8, -5)
    strided = 128 + 4 * (n % 8) + (n - 192) // 8
    q_slot = jnp.where(n < 128, n, jnp.where(n < 192, late, strided)).astype(F32)
    q_spots = jnp.where(q_slot == query_slot, 1.0, 0.0).astype(BF16)
    query = dot_nn(q_spots, mine).astype(BF16)
    key = dot_nn(kv_spots, key).astype(BF16)
    values[...] = dot_nn(kv_spots, value).astype(BF16)

    main = dot_nt(query[:192], key[:128]) * scale
    tail = dot_nt(query[192:], key[128:]) * scale
    lane = iota((8, HEAD_DIM), 1) // 32
    packed = jnp.zeros((8, HEAD_DIM), F32)
    for j in range(4):
        packed = jnp.where(lane == j, tail[8 * j : 8 * j + 8], packed)
    out[:SHORT] = main[:128].reshape(SHORT, 8, 128)
    long = main[128:].reshape(8, 8, 128)
    fifth = iota(long.shape, 1) == 4
    out[SHORT:] = jnp.where(fifth, jnp.broadcast_to(packed[:, None, :], long.shape), long)


def spread(coefs, table):
    for j in range(HEADS):
        table[j] = jnp.broadcast_to(coefs[:, j : j + 1], (HEADS, 128))


def mix(table, terms):
    sums = []
    for j in range(HEADS):
        total = table[j, 0:1, :] * terms[0]
        for h in range(1, HEADS):
            total = total + table[j, h : h + 1, :] * terms[h]
        sums.append(total)
    return jnp.stack(sums)


def soften_kernel(logits, table_b, table_a, info, out):
    owner = lax.axis_index("grp") * GROUP + lax.axis_index("sub")
    shard = lax.axis_index("seq").astype(F32)
    is_long = owner >= SHORT
    line = iota((8, 128), 0)
    lane = iota((8, 128), 1)
    slot = jnp.where(is_long, 128 + 4 * (owner - SHORT), 8 * owner) + line
    valid = jnp.logical_or(line < 4, jnp.logical_not(is_long))
    begin, length, own = info[0:1, :], info[1:2, :], info[2:3, :]
    slot_f = slot.astype(F32)
    held = (own == shard) & (slot_f >= begin) & (slot_f < begin + length) & valid
    filled = jnp.sum(jnp.where(held, 1.0, 0.0), axis=1, keepdims=True) > 0.5
    first = jnp.sum(jnp.where(held, begin, 0.0), axis=1, keepdims=True)

    def allowed(other):
        other_f = other.astype(F32)
        return (other_f >= first) & (other_f <= slot_f) & filled

    main_ok = allowed(lane)
    tail_ok = allowed(128 + lane % 32) & is_long & (lane // 32 == line)
    mixed = mix(table_b, [logits[h] for h in range(HEADS)])
    tail = jnp.broadcast_to(mixed[:, 4:5, :], mixed.shape)
    main_m = jnp.where(main_ok[None], mixed, -1e30)
    tail_m = jnp.where(tail_ok[None], tail, -1e30)
    top = jnp.max(jnp.maximum(main_m, tail_m), axis=2, keepdims=True)
    main_e = jnp.where(main_ok[None], jnp.exp(main_m - top), 0.0)
    tail_e = jnp.where(tail_ok[None], jnp.exp(tail_m - top), 0.0)
    total = jnp.sum(main_e + tail_e, axis=2, keepdims=True)
    share = 1.0 / jnp.where(filled[None], total, 1.0)
    main_w = (main_e * share).astype(BF16).astype(F32)
    tail_w = (tail_e * share).astype(BF16).astype(F32)
    tail_w = jnp.broadcast_to(jnp.sum(tail_w, axis=1, keepdims=True), tail_w.shape)
    weights = jnp.where(((line == 4) & is_long)[None], tail_w, main_w)
    out[...] = mix(table_a, [weights[h] for h in range(HEADS)]).astype(BF16)


def output_kernel(weights, values, out):
    out[:128, :] = dot_nn(weights[:128, :], values[:128, :]).astype(BF16)
    long = weights[128:, :].astype(F32).reshape(8, 8, 128)
    tail = jnp.broadcast_to(long[:, 4:5, :], long.shape)
    tail = jnp.where(iota(long.shape, 2) // 32 == iota(long.shape, 1), tail, 0.0)
    rows = dot_nn(weights[128:, :], values[:128, :]) + dot_nn(
        tail.reshape(64, 128).astype(BF16), values[128:, :]
    )
    for i in range(8):
        out[128 + 4 * i : 132 + 4 * i, :] = rows[8 * i : 8 * i + 4, :].astype(BF16)


def on_device(
    hidden, w_query, w_key, w_value, mix_before, mix_after, doc_lengths, doc_owner, loader_order
):
    depth = hidden.shape[1]
    grant = pltpu.CompilerParams(vmem_limit_bytes=12 << 20)
    packed = pltpu.CompilerParams(
        vmem_limit_bytes=12 << 20
    )
    rows = N_SEQ * PIECE
    vmem = pl.BlockSpec(memory_space=pltpu.VMEM)
    pair = np.arange(HEAD_DIM) // 2
    freq = jnp.asarray((THETA ** (-2.0 * pair / HEAD_DIM)).astype(np.float32)[None, :])
    lens = doc_lengths.reshape(1, TOK)
    own = doc_owner.reshape(1, TOK)
    order = loader_order.reshape(N_SEQ, TOK)

    hbm = pl.BlockSpec(memory_space=pltpu.HBM)
    table = jax.ShapeDtypeStruct((HEADS, HEADS, 128), F32)
    send, info, table_b, table_a = pl.pallas_call(
        project_kernel,
        in_specs=[hbm] * 10,
        out_specs=[vmem] * 4,
        out_shape=[
            jax.ShapeDtypeStruct((rows, HEAD_DIM), BF16),
            jax.ShapeDtypeStruct((8, TOK), F32),
            table,
            table,
        ],
        scratch_shapes=[
            pltpu.VMEM((TOK, depth), BF16),
            pltpu.VMEM((depth, HEAD_DIM), BF16),
            pltpu.VMEM((4 * KV_COLS, depth), BF16),
            pltpu.VMEM((1, TOK), jnp.int32),
            pltpu.VMEM((1, TOK), jnp.int32),
            pltpu.VMEM((N_SEQ, TOK), jnp.int32),
            pltpu.VMEM((1, TOK), F32),
            pltpu.VMEM((TOK, HEAD_DIM), F32),
            pltpu.VMEM((TOK, HEAD_DIM), F32),
            pltpu.VMEM((2, TOK, HEAD_DIM), F32),
            pltpu.VMEM((rows, 3 * TOK), BF16),
            pltpu.VMEM((HEADS, HEADS), F32),
            pltpu.VMEM((HEADS, HEADS), F32),
            pltpu.SemaphoreType.DMA((14,)),
        ],
        compiler_params=packed,
        name="project",
    )(
        *[
            pltpu.with_memory_space_constraint(x, pltpu.HBM)
            for x in (
                hidden, w_query, w_key.T, w_value.T, lens, own, order, freq, mix_before, mix_after,
            )
        ]
    )

    got = lax.all_to_all(
        send.reshape(N_SEQ, PIECE, HEAD_DIM), "seq", split_axis=0, concat_axis=0, tiled=True
    )
    gathered = lax.all_gather(got[:, PIECE - KV_ROWS :], "sub", axis=0, tiled=True)
    got = got.reshape(rows, HEAD_DIM)
    gathered = gathered.reshape(GROUP * N_SEQ * KV_ROWS, HEAD_DIM)

    logits, values = pl.pallas_call(
        functools.partial(logits_kernel, 1.0 / HEAD_DIM**0.5),
        in_specs=[vmem, vmem],
        out_specs=[vmem, vmem],
        out_shape=[
            jax.ShapeDtypeStruct((HEADS, 8, 128), F32),
            jax.ShapeDtypeStruct((rows, HEAD_DIM), BF16),
        ],
        compiler_params=packed,
        name="logits",
    )(got, gathered)

    mine = lax.all_to_all(logits, ("grp", "sub"), split_axis=0, concat_axis=0, tiled=True)
    blended = pl.pallas_call(
        soften_kernel,
        in_specs=[vmem] * 4,
        out_specs=vmem,
        out_shape=jax.ShapeDtypeStruct((HEADS, 8, 128), BF16),
        compiler_params=grant,
        name="soften",
    )(mine, table_b, table_a, info)
    back = lax.all_to_all(blended, ("grp", "sub"), split_axis=0, concat_axis=0, tiled=True)
    return pl.pallas_call(
        output_kernel,
        in_specs=[vmem, vmem],
        out_specs=vmem,
        out_shape=jax.ShapeDtypeStruct((CAP, HEAD_DIM), BF16),
        compiler_params=grant,
        name="output",
    )(back.reshape(HEADS * 8, 128), values)


def solution(mesh):
    split = Mesh(mesh.devices.reshape(N_SEQ, HEADS // GROUP, GROUP), ("seq", "grp", "sub"))
    mp = ("grp", "sub")
    placed = (P("seq", None), P(None, mp), P(None, mp), P(None, mp), P(), P(), P(), P(), P())
    return jax.shard_map(
        on_device, mesh=split, in_specs=placed, out_specs=P("seq", mp), check_vma=False
    )
```

```python
import functools

import jax
import jax.numpy as jnp
import numpy as np
from jax import lax
from jax.experimental import pallas as pl
from jax.experimental.pallas import tpu as pltpu
from jax.sharding import Mesh
from jax.sharding import PartitionSpec as P

THETA = 500000.0
N_SEQ = 32
HEADS = 24
GROUP = 4
HEAD_DIM = 128
KV_COLS = 32
TOK = 128
CAP = 160
PIECE = 8
KV_ROW = 5
KV_ROWS = 4
META = 7
SHORT = 16
F32 = jnp.float32
BF16 = jnp.bfloat16


def iota(shape, dim):
    return lax.broadcasted_iota(jnp.int32, shape, dim)


def dot_nt(a, b):
    return lax.dot_general(a, b, (((1,), (1,)), ((), ())), preferred_element_type=F32)


def dot_nn(a, b):
    return lax.dot_general(a, b, (((1,), (0,)), ((), ())), preferred_element_type=F32)


def turn(shape, sub):
    return (iota(shape, len(shape) - 1) - KV_COLS * sub) & (HEAD_DIM - 1)


def project_kernel(
    hid_h, wq_h, wk_h, wv_h, lens_h, own_h, order_h, freq_h, before_h, after_h,
    send, info, table_b, table_a,
    hid, wq, wkv, lens, own, order, freq, cos_t, sin_t, first, place, before, after, sems,
):
    sub = lax.axis_index("sub")
    copies = []

    def copy(source, target):
        copies.append(pltpu.make_async_copy(source, target, sems.at[len(copies)]))
        copies[-1].start()

    copy(lens_h, lens)
    copy(own_h, own)
    copy(order_h, order)
    copy(freq_h, freq)
    half = hid.shape[1] // 2
    for part in range(2):
        span = pl.ds(part * half, half)
        copy(hid_h.at[:, span], hid.at[:, span])
        copy(wq_h.at[span, :], wq.at[span, :])
        copy(wk_h.at[:, span], wkv.at[pl.ds(0, KV_COLS), span])
        copy(wv_h.at[:, span], wkv.at[pl.ds(KV_COLS, KV_COLS), span])
        if part == 0:
            copy(before_h, before)
            copy(after_h, after)
    wkv[2 * KV_COLS :, :] = jnp.zeros((2 * KV_COLS, hid.shape[1]), BF16)
    for c in copies[:4]:
        c.wait()

    shape = (TOK, TOK)
    row, col = iota(shape, 0), iota(shape, 1)
    eye = row == col
    low = row < col

    def down(value):
        return jnp.sum(jnp.where(eye, value, 0.0), axis=1, keepdims=True)

    def across(value):
        return jnp.sum(jnp.where(eye, value, 0.0), axis=0, keepdims=True)

    len_row = lens[...].astype(F32)
    own_row = own[...].astype(F32)
    len_col, own_col = down(len_row), down(own_row)
    start = jnp.sum(jnp.where(low, len_col, 0.0), axis=0, keepdims=True)
    shard_start = jnp.sum(
        jnp.where(low & (own_col == own_row), len_col, 0.0), axis=0, keepdims=True
    )
    line = iota((8, TOK), 0)
    info[...] = jnp.where(line == 0, shard_start, jnp.where(line == 1, len_row, own_row))
    packed = down(order[pl.ds(lax.axis_index("seq"), 1), :].astype(F32))
    inside = (packed >= start) & (packed < start + len_row)

    def pick(value):
        return jnp.sum(jnp.where(inside, value, 0.0), axis=1, keepdims=True)

    target = pick(own_row)
    position = packed - pick(start)
    slot = pick(shard_start) + position
    target_row = across(target)
    rank = jnp.sum(
        jnp.where((target_row == target) & (col < row), 1.0, 0.0), axis=1, keepdims=True
    )
    pair = jnp.floor(rank * 0.5)
    angle = position * freq[...]
    cos_t[...] = jnp.cos(angle)
    even = col % 2 == 0
    sin = jnp.sin(angle)
    sin_t[...] = jnp.where(even, -sin, sin)
    rows = iota((N_SEQ * PIECE, TOK), 0).astype(F32)

    def put(k, where_to):
        place[:, k * TOK : (k + 1) * TOK] = jnp.where(rows == where_to, 1.0, 0.0).astype(BF16)

    put(0, across(target * PIECE + rank))
    put(1, target_row * PIECE + META)
    put(2, across(target * PIECE + KV_ROW + pair))
    turned = turn(shape, sub)
    meta = turned.astype(F32) == rank + HEAD_DIM // 2
    meta = jnp.where(meta, slot + 1.0, 0.0).astype(BF16)
    side = (turned // (HEAD_DIM // 2)).astype(F32) == rank - 2.0 * pair

    for c in copies[4:10]:
        c.wait()
    first[0] = dot_nn(hid[:, :half], wq[:half, :])
    first[1] = dot_nt(hid[:, :half], wkv[:, :half])
    spread(before, table_b)
    spread(after, table_a)
    for c in copies[10:]:
        c.wait()
    acc_q = first[0] + dot_nn(hid[:, half:], wq[half:, :])
    acc_kv = first[1] + dot_nt(hid[:, half:], wkv[:, half:])
    even = col % 2 == 0

    cos_a, sin_a = cos_t[...], sin_t[...]

    def rope(value):
        partner = jnp.where(even, pltpu.roll(value, HEAD_DIM - 1, 1), pltpu.roll(value, 1, 1))
        return value * cos_a + partner * sin_a

    query = rope(acc_q).astype(BF16)
    kv = pltpu.roll(acc_kv, KV_COLS * sub, 1)
    kv = jnp.where(turned < KV_COLS, rope(kv), kv)
    kv = jnp.where(side, kv + pltpu.roll(kv, HEAD_DIM // 2, 1), 0.0).astype(BF16)
    moved = dot_nn(place[:, : 2 * TOK], jnp.concatenate([query, meta], axis=0))
    send[...] = (moved + dot_nn(place[:, 2 * TOK :], kv)).astype(BF16)


def logits_kernel(scale, got, gathered, out, values):
    rows = N_SEQ * PIECE
    mine = got[...]
    head = mine.astype(F32).reshape(N_SEQ, PIECE, HEAD_DIM)
    tags = jnp.broadcast_to(head[:, META : META + 1, :], head.shape)
    line, lane = iota(head.shape, 1), turn(head.shape, lax.axis_index("sub")) - HEAD_DIM // 2
    token = jnp.where(line < KV_ROW, line, 2 * (line - KV_ROW))
    weight = jnp.where((lane == token + 1) & (line >= KV_ROW) & (line < META), 256.0, 0.0)
    weight = jnp.where(lane == token, 1.0, weight)
    column = jnp.sum(weight * tags, axis=2, keepdims=True).reshape(rows, 1)

    def across(shape, target):
        hit = iota(shape, 0) == target
        return jnp.sum(jnp.where(hit, column, 0.0), axis=0, keepdims=True)

    n = iota((rows, rows), 1)
    query_slot = across((rows, rows), jnp.where(n % PIECE < KV_ROW, n, -1)) - 1.0
    kv_rows = N_SEQ * KV_ROWS
    n = iota((rows, kv_rows), 1)
    n = jnp.where(n % KV_ROWS > 0, n // KV_ROWS * PIECE + PIECE - KV_ROWS + n % KV_ROWS, -1)
    both = across((rows, kv_rows), n)
    right = jnp.floor(both * (1.0 / 256.0))
    left, right = both - 256.0 * right - 1.0, right - 1.0

    window = iota((kv_rows, HEAD_DIM), 1) // KV_COLS
    blocks = [jnp.zeros((kv_rows, HEAD_DIM), F32)] * 4
    for c in range(GROUP):
        tile = gathered[c * kv_rows : (c + 1) * kv_rows, :].astype(F32)
        for i in range(4):
            blocks[i] = jnp.where(window == (c + i) % GROUP, tile, blocks[i])
    for i in range(1, 4):
        blocks[i] = pltpu.roll(blocks[i], HEAD_DIM - i * KV_COLS, 1)
    key = jnp.concatenate([blocks[0].astype(BF16), blocks[2].astype(BF16)], axis=0)
    value = jnp.concatenate([blocks[1].astype(BF16), blocks[3].astype(BF16)], axis=0)

    n = iota((rows, 1), 0)
    kv_slot = jnp.where(n < 128, n, 128 + n % 32).astype(F32)
    from_left = jnp.where(kv_slot == left, 1.0, 0.0).astype(BF16)
    from_right = jnp.where(kv_slot == right, 1.0, 0.0).astype(BF16)
    kv_spots = jnp.concatenate([from_left, from_right], axis=1)
    n = iota((224, 1), 0)
    late = jnp.where(n % 8 < 4, 64 + n // 8 * 4 + n % 8, -5)
    strided = 128 + 4 * (n % 8) + (n - 192) // 8
    q_slot = jnp.where(n < 128, n, jnp.where(n < 192, late, strided)).astype(F32)
    q_spots = jnp.where(q_slot == query_slot, 1.0, 0.0).astype(BF16)
    query = dot_nn(q_spots, mine).astype(BF16)
    key = dot_nn(kv_spots, key).astype(BF16)
    values[...] = dot_nn(kv_spots, value).astype(BF16)

    main = dot_nt(query[:192], key[:128]) * scale
    tail = dot_nt(query[192:], key[128:]) * scale
    lane = iota((8, HEAD_DIM), 1) // 32
    packed = jnp.zeros((8, HEAD_DIM), F32)
    for j in range(4):
        packed = jnp.where(lane == j, tail[8 * j : 8 * j + 8], packed)
    out[:SHORT] = main[:128].reshape(SHORT, 8, 128)
    long = main[128:].reshape(8, 8, 128)
    fifth = iota(long.shape, 1) == 4
    out[SHORT:] = jnp.where(fifth, jnp.broadcast_to(packed[:, None, :], long.shape), long)


def spread(coefs, table):
    for j in range(HEADS):
        table[j] = jnp.broadcast_to(coefs[:, j : j + 1], (HEADS, 128))


def mix(table, terms):
    sums = []
    for j in range(HEADS):
        total = table[j, 0:1, :] * terms[0]
        for h in range(1, HEADS):
            total = total + table[j, h : h + 1, :] * terms[h]
        sums.append(total)
    return jnp.stack(sums)


def soften_kernel(logits, table_b, table_a, info, out):
    owner = lax.axis_index("grp") * GROUP + lax.axis_index("sub")
    shard = lax.axis_index("seq").astype(F32)
    is_long = owner >= SHORT
    line = iota((8, 128), 0)
    lane = iota((8, 128), 1)
    slot = jnp.where(is_long, 128 + 4 * (owner - SHORT), 8 * owner) + line
    valid = jnp.logical_or(line < 4, jnp.logical_not(is_long))
    begin, length, own = info[0:1, :], info[1:2, :], info[2:3, :]
    slot_f = slot.astype(F32)
    held = (own == shard) & (slot_f >= begin) & (slot_f < begin + length) & valid
    filled = jnp.sum(jnp.where(held, 1.0, 0.0), axis=1, keepdims=True) > 0.5
    first = jnp.sum(jnp.where(held, begin, 0.0), axis=1, keepdims=True)

    def allowed(other):
        other_f = other.astype(F32)
        return (other_f >= first) & (other_f <= slot_f) & filled

    main_ok = allowed(lane)
    tail_ok = allowed(128 + lane % 32) & is_long & (lane // 32 == line)
    mixed = mix(table_b, [logits[h] for h in range(HEADS)])
    tail = jnp.broadcast_to(mixed[:, 4:5, :], mixed.shape)
    main_m = jnp.where(main_ok[None], mixed, -1e30)
    tail_m = jnp.where(tail_ok[None], tail, -1e30)
    top = jnp.max(jnp.maximum(main_m, tail_m), axis=2, keepdims=True)
    main_e = jnp.where(main_ok[None], jnp.exp(main_m - top), 0.0)
    tail_e = jnp.where(tail_ok[None], jnp.exp(tail_m - top), 0.0)
    total = jnp.sum(main_e + tail_e, axis=2, keepdims=True)
    share = 1.0 / jnp.where(filled[None], total, 1.0)
    main_w = (main_e * share).astype(BF16).astype(F32)
    tail_w = (tail_e * share).astype(BF16).astype(F32)
    tail_w = jnp.broadcast_to(jnp.sum(tail_w, axis=1, keepdims=True), tail_w.shape)
    weights = jnp.where(((line == 4) & is_long)[None], tail_w, main_w)
    out[...] = mix(table_a, [weights[h] for h in range(HEADS)]).astype(BF16)


def output_kernel(weights, values, out):
    out[:128, :] = dot_nn(weights[:128, :], values[:128, :]).astype(BF16)
    long = weights[128:, :].astype(F32).reshape(8, 8, 128)
    tail = jnp.broadcast_to(long[:, 4:5, :], long.shape)
    tail = jnp.where(iota(long.shape, 2) // 32 == iota(long.shape, 1), tail, 0.0)
    rows = dot_nn(weights[128:, :], values[:128, :]) + dot_nn(
        tail.reshape(64, 128).astype(BF16), values[128:, :]
    )
    for i in range(8):
        out[128 + 4 * i : 132 + 4 * i, :] = rows[8 * i : 8 * i + 4, :].astype(BF16)


def on_device(
    hidden, w_query, w_key, w_value, mix_before, mix_after, doc_lengths, doc_owner, loader_order
):
    depth = hidden.shape[1]
    grant = pltpu.CompilerParams(vmem_limit_bytes=12 << 20)
    packed = pltpu.CompilerParams(
        vmem_limit_bytes=12 << 20
    )
    rows = N_SEQ * PIECE
    vmem = pl.BlockSpec(memory_space=pltpu.VMEM)
    pair = np.arange(HEAD_DIM) // 2
    freq = jnp.asarray((THETA ** (-2.0 * pair / HEAD_DIM)).astype(np.float32)[None, :])
    lens = doc_lengths.reshape(1, TOK)
    own = doc_owner.reshape(1, TOK)
    order = loader_order.reshape(N_SEQ, TOK)

    hbm = pl.BlockSpec(memory_space=pltpu.HBM)
    table = jax.ShapeDtypeStruct((HEADS, HEADS, 128), F32)
    send, info, table_b, table_a = pl.pallas_call(
        project_kernel,
        in_specs=[hbm] * 10,
        out_specs=[vmem] * 4,
        out_shape=[
            jax.ShapeDtypeStruct((rows, HEAD_DIM), BF16),
            jax.ShapeDtypeStruct((8, TOK), F32),
            table,
            table,
        ],
        scratch_shapes=[
            pltpu.VMEM((TOK, depth), BF16),
            pltpu.VMEM((depth, HEAD_DIM), BF16),
            pltpu.VMEM((4 * KV_COLS, depth), BF16),
            pltpu.VMEM((1, TOK), jnp.int32),
            pltpu.VMEM((1, TOK), jnp.int32),
            pltpu.VMEM((N_SEQ, TOK), jnp.int32),
            pltpu.VMEM((1, TOK), F32),
            pltpu.VMEM((TOK, HEAD_DIM), F32),
            pltpu.VMEM((TOK, HEAD_DIM), F32),
            pltpu.VMEM((2, TOK, HEAD_DIM), F32),
            pltpu.VMEM((rows, 3 * TOK), BF16),
            pltpu.VMEM((HEADS, HEADS), F32),
            pltpu.VMEM((HEADS, HEADS), F32),
            pltpu.SemaphoreType.DMA((14,)),
        ],
        compiler_params=packed,
        name="project",
    )(
        *[
            pltpu.with_memory_space_constraint(x, pltpu.HBM)
            for x in (
                hidden, w_query, w_key.T, w_value.T, lens, own, order, freq, mix_before, mix_after,
            )
        ]
    )

    got = lax.all_to_all(
        send.reshape(N_SEQ, PIECE, HEAD_DIM), "seq", split_axis=0, concat_axis=0, tiled=True
    )
    gathered = lax.all_gather(got[:, PIECE - KV_ROWS :], "sub", axis=0, tiled=True)
    got = got.reshape(rows, HEAD_DIM)
    gathered = gathered.reshape(GROUP * N_SEQ * KV_ROWS, HEAD_DIM)

    logits, values = pl.pallas_call(
        functools.partial(logits_kernel, 1.0 / HEAD_DIM**0.5),
        in_specs=[vmem, vmem],
        out_specs=[vmem, vmem],
        out_shape=[
            jax.ShapeDtypeStruct((HEADS, 8, 128), F32),
            jax.ShapeDtypeStruct((rows, HEAD_DIM), BF16),
        ],
        compiler_params=packed,
        name="logits",
    )(got, gathered)

    mine = lax.all_to_all(logits, ("grp", "sub"), split_axis=0, concat_axis=0, tiled=True)
    blended = pl.pallas_call(
        soften_kernel,
        in_specs=[vmem] * 4,
        out_specs=vmem,
        out_shape=jax.ShapeDtypeStruct((HEADS, 8, 128), BF16),
        compiler_params=grant,
        name="soften",
    )(mine, table_b, table_a, info)
    back = lax.all_to_all(blended, ("grp", "sub"), split_axis=0, concat_axis=0, tiled=True)
    return pl.pallas_call(
        output_kernel,
        in_specs=[vmem, vmem],
        out_specs=vmem,
        out_shape=jax.ShapeDtypeStruct((CAP, HEAD_DIM), BF16),
        compiler_params=grant,
        name="output",
    )(back.reshape(HEADS * 8, 128), values)


def solution(mesh):
    split = Mesh(mesh.devices.reshape(N_SEQ, HEADS // GROUP, GROUP), ("seq", "grp", "sub"))
    mp = ("grp", "sub")
    placed = (P("seq", None), P(None, mp), P(None, mp), P(None, mp), P(), P(), P(), P(), P())
    return jax.shard_map(
        on_device, mesh=split, in_specs=placed, out_specs=P("seq", mp), check_vma=False
    )
```

```python
import functools

import jax
import jax.numpy as jnp
import numpy as np
from jax import lax
from jax.experimental import pallas as pl
from jax.experimental.pallas import tpu as pltpu
from jax.sharding import Mesh
from jax.sharding import PartitionSpec as P

THETA = 500000.0
N_SEQ = 32
HEADS = 24
GROUP = 4
HEAD_DIM = 128
KV_COLS = 32
TOK = 128
CAP = 160
PIECE = 8
KV_ROW = 5
KV_ROWS = 4
META = 7
SHORT = 16
F32 = jnp.float32
BF16 = jnp.bfloat16


def iota(shape, dim):
    return lax.broadcasted_iota(jnp.int32, shape, dim)


def dot_nt(a, b):
    return lax.dot_general(a, b, (((1,), (1,)), ((), ())), preferred_element_type=F32)


def dot_nn(a, b):
    return lax.dot_general(a, b, (((1,), (0,)), ((), ())), preferred_element_type=F32)


def turn(shape, sub):
    return (iota(shape, len(shape) - 1) - KV_COLS * sub) & (HEAD_DIM - 1)


def project_kernel(
    hid_h, wq_h, wk_h, wv_h, lens_h, own_h, order_h, freq_h, before_h, after_h,
    send, info, table_b, table_a,
    hid, wq, wkv, lens, own, order, freq, cos_t, sin_t, first, place, before, after, sems,
):
    sub = lax.axis_index("sub")
    copies = []

    def copy(source, target):
        copies.append(pltpu.make_async_copy(source, target, sems.at[len(copies)]))
        copies[-1].start()

    copy(lens_h, lens)
    copy(own_h, own)
    copy(order_h, order)
    copy(freq_h, freq)
    copy(before_h, before)
    copy(after_h, after)
    half = hid.shape[1] // 2
    for part in range(2):
        span = pl.ds(part * half, half)
        copy(hid_h.at[:, span], hid.at[:, span])
        copy(wq_h.at[span, :], wq.at[span, :])
        copy(wk_h.at[:, span], wkv.at[pl.ds(0, KV_COLS), span])
        copy(wv_h.at[:, span], wkv.at[pl.ds(KV_COLS, KV_COLS), span])
    wkv[2 * KV_COLS :, :] = jnp.zeros((2 * KV_COLS, hid.shape[1]), BF16)
    for c in copies[:6]:
        c.wait()

    shape = (TOK, TOK)
    row, col = iota(shape, 0), iota(shape, 1)
    eye = row == col
    low = row < col

    def down(value):
        return jnp.sum(jnp.where(eye, value, 0.0), axis=1, keepdims=True)

    def across(value):
        return jnp.sum(jnp.where(eye, value, 0.0), axis=0, keepdims=True)

    len_row = lens[...].astype(F32)
    own_row = own[...].astype(F32)
    len_col, own_col = down(len_row), down(own_row)
    start = jnp.sum(jnp.where(low, len_col, 0.0), axis=0, keepdims=True)
    shard_start = jnp.sum(
        jnp.where(low & (own_col == own_row), len_col, 0.0), axis=0, keepdims=True
    )
    line = iota((8, TOK), 0)
    info[...] = jnp.where(line == 0, shard_start, jnp.where(line == 1, len_row, own_row))
    packed = down(order[pl.ds(lax.axis_index("seq"), 1), :].astype(F32))
    inside = (packed >= start) & (packed < start + len_row)

    def pick(value):
        return jnp.sum(jnp.where(inside, value, 0.0), axis=1, keepdims=True)

    target = pick(own_row)
    position = packed - pick(start)
    slot = pick(shard_start) + position
    target_row = across(target)
    rank = jnp.sum(
        jnp.where((target_row == target) & (col < row), 1.0, 0.0), axis=1, keepdims=True
    )
    pair = jnp.floor(rank * 0.5)
    angle = position * freq[...]
    cos_t[...] = jnp.cos(angle)
    even = col % 2 == 0
    sin = jnp.sin(angle)
    sin_t[...] = jnp.where(even, -sin, sin)
    rows = iota((N_SEQ * PIECE, TOK), 0).astype(F32)

    def put(k, where_to):
        place[:, k * TOK : (k + 1) * TOK] = jnp.where(rows == where_to, 1.0, 0.0).astype(BF16)

    put(0, across(target * PIECE + rank))
    put(1, target_row * PIECE + META)
    put(2, across(target * PIECE + KV_ROW + pair))
    turned = turn(shape, sub)
    meta = turned.astype(F32) == rank + HEAD_DIM // 2
    meta = jnp.where(meta, slot + 1.0, 0.0).astype(BF16)
    side = (turned // (HEAD_DIM // 2)).astype(F32) == rank - 2.0 * pair

    for c in copies[6:10]:
        c.wait()
    first[0] = dot_nn(hid[:, :half], wq[:half, :])
    first[1] = dot_nt(hid[:, :half], wkv[:, :half])
    spread(before, table_b)
    spread(after, table_a)
    for c in copies[10:]:
        c.wait()
    acc_q = first[0] + dot_nn(hid[:, half:], wq[half:, :])
    acc_kv = first[1] + dot_nt(hid[:, half:], wkv[:, half:])
    even = col % 2 == 0

    cos_a, sin_a = cos_t[...], sin_t[...]

    def rope(value):
        partner = jnp.where(even, pltpu.roll(value, HEAD_DIM - 1, 1), pltpu.roll(value, 1, 1))
        return value * cos_a + partner * sin_a

    query = rope(acc_q).astype(BF16)
    kv = pltpu.roll(acc_kv, KV_COLS * sub, 1)
    kv = jnp.where(turned < KV_COLS, rope(kv), kv)
    kv = jnp.where(side, kv + pltpu.roll(kv, HEAD_DIM // 2, 1), 0.0).astype(BF16)
    moved = dot_nn(place[:, : 2 * TOK], jnp.concatenate([query, meta], axis=0))
    send[...] = (moved + dot_nn(place[:, 2 * TOK :], kv)).astype(BF16)


def logits_kernel(scale, got, gathered, out, values):
    rows = N_SEQ * PIECE
    mine = got[...]
    head = mine.astype(F32).reshape(N_SEQ, PIECE, HEAD_DIM)
    tags = jnp.broadcast_to(head[:, META : META + 1, :], head.shape)
    line, lane = iota(head.shape, 1), turn(head.shape, lax.axis_index("sub")) - HEAD_DIM // 2
    token = jnp.where(line < KV_ROW, line, 2 * (line - KV_ROW))
    weight = jnp.where((lane == token + 1) & (line >= KV_ROW) & (line < META), 256.0, 0.0)
    weight = jnp.where(lane == token, 1.0, weight)
    column = jnp.sum(weight * tags, axis=2, keepdims=True).reshape(rows, 1)

    def across(shape, target):
        hit = iota(shape, 0) == target
        return jnp.sum(jnp.where(hit, column, 0.0), axis=0, keepdims=True)

    n = iota((rows, rows), 1)
    query_slot = across((rows, rows), jnp.where(n % PIECE < KV_ROW, n, -1)) - 1.0
    kv_rows = N_SEQ * KV_ROWS
    n = iota((rows, kv_rows), 1)
    n = jnp.where(n % KV_ROWS > 0, n // KV_ROWS * PIECE + PIECE - KV_ROWS + n % KV_ROWS, -1)
    both = across((rows, kv_rows), n)
    right = jnp.floor(both * (1.0 / 256.0))
    left, right = both - 256.0 * right - 1.0, right - 1.0

    window = iota((kv_rows, HEAD_DIM), 1) // KV_COLS
    blocks = [jnp.zeros((kv_rows, HEAD_DIM), F32)] * 4
    for c in range(GROUP):
        tile = gathered[c * kv_rows : (c + 1) * kv_rows, :].astype(F32)
        for i in range(4):
            blocks[i] = jnp.where(window == (c + i) % GROUP, tile, blocks[i])
    for i in range(1, 4):
        blocks[i] = pltpu.roll(blocks[i], HEAD_DIM - i * KV_COLS, 1)
    key = jnp.concatenate([blocks[0].astype(BF16), blocks[2].astype(BF16)], axis=0)
    value = jnp.concatenate([blocks[1].astype(BF16), blocks[3].astype(BF16)], axis=0)

    n = iota((rows, 1), 0)
    kv_slot = jnp.where(n < 128, n, 128 + n % 32).astype(F32)
    from_left = jnp.where(kv_slot == left, 1.0, 0.0).astype(BF16)
    from_right = jnp.where(kv_slot == right, 1.0, 0.0).astype(BF16)
    kv_spots = jnp.concatenate([from_left, from_right], axis=1)
    n = iota((224, 1), 0)
    late = jnp.where(n % 8 < 4, 64 + n // 8 * 4 + n % 8, -5)
    strided = 128 + 4 * (n % 8) + (n - 192) // 8
    q_slot = jnp.where(n < 128, n, jnp.where(n < 192, late, strided)).astype(F32)
    q_spots = jnp.where(q_slot == query_slot, 1.0, 0.0).astype(BF16)
    query = dot_nn(q_spots, mine).astype(BF16)
    key = dot_nn(kv_spots, key).astype(BF16)
    values[...] = dot_nn(kv_spots, value).astype(BF16)

    main = dot_nt(query[:192], key[:128]) * scale
    tail = dot_nt(query[192:], key[128:]) * scale
    lane = iota((8, HEAD_DIM), 1) // 32
    packed = jnp.zeros((8, HEAD_DIM), F32)
    for j in range(4):
        packed = jnp.where(lane == j, tail[8 * j : 8 * j + 8], packed)
    out[:SHORT] = main[:128].reshape(SHORT, 8, 128)
    long = main[128:].reshape(8, 8, 128)
    fifth = iota(long.shape, 1) == 4
    out[SHORT:] = jnp.where(fifth, jnp.broadcast_to(packed[:, None, :], long.shape), long)


def spread(coefs, table):
    for j in range(HEADS):
        table[j] = jnp.broadcast_to(coefs[:, j : j + 1], (HEADS, 128))


def mix(table, terms):
    sums = []
    for j in range(HEADS):
        total = table[j, 0:1, :] * terms[0]
        for h in range(1, HEADS):
            total = total + table[j, h : h + 1, :] * terms[h]
        sums.append(total)
    return jnp.stack(sums)


def soften_kernel(logits, table_b, table_a, info, out):
    owner = lax.axis_index("grp") * GROUP + lax.axis_index("sub")
    shard = lax.axis_index("seq").astype(F32)
    is_long = owner >= SHORT
    line = iota((8, 128), 0)
    lane = iota((8, 128), 1)
    slot = jnp.where(is_long, 128 + 4 * (owner - SHORT), 8 * owner) + line
    valid = jnp.logical_or(line < 4, jnp.logical_not(is_long))
    begin, length, own = info[0:1, :], info[1:2, :], info[2:3, :]
    slot_f = slot.astype(F32)
    held = (own == shard) & (slot_f >= begin) & (slot_f < begin + length) & valid
    filled = jnp.sum(jnp.where(held, 1.0, 0.0), axis=1, keepdims=True) > 0.5
    first = jnp.sum(jnp.where(held, begin, 0.0), axis=1, keepdims=True)

    def allowed(other):
        other_f = other.astype(F32)
        return (other_f >= first) & (other_f <= slot_f) & filled

    main_ok = allowed(lane)
    tail_ok = allowed(128 + lane % 32) & is_long & (lane // 32 == line)
    mixed = mix(table_b, [logits[h] for h in range(HEADS)])
    tail = jnp.broadcast_to(mixed[:, 4:5, :], mixed.shape)
    main_m = jnp.where(main_ok[None], mixed, -1e30)
    tail_m = jnp.where(tail_ok[None], tail, -1e30)
    top = jnp.max(jnp.maximum(main_m, tail_m), axis=2, keepdims=True)
    main_e = jnp.where(main_ok[None], jnp.exp(main_m - top), 0.0)
    tail_e = jnp.where(tail_ok[None], jnp.exp(tail_m - top), 0.0)
    total = jnp.sum(main_e + tail_e, axis=2, keepdims=True)
    share = 1.0 / jnp.where(filled[None], total, 1.0)
    main_w = (main_e * share).astype(BF16).astype(F32)
    tail_w = (tail_e * share).astype(BF16).astype(F32)
    tail_w = jnp.broadcast_to(jnp.sum(tail_w, axis=1, keepdims=True), tail_w.shape)
    weights = jnp.where(((line == 4) & is_long)[None], tail_w, main_w)
    out[...] = mix(table_a, [weights[h] for h in range(HEADS)]).astype(BF16)


def output_kernel(weights, values, out):
    out[:128, :] = dot_nn(weights[:128, :], values[:128, :]).astype(BF16)
    long = weights[128:, :].astype(F32).reshape(8, 8, 128)
    tail = jnp.broadcast_to(long[:, 4:5, :], long.shape)
    tail = jnp.where(iota(long.shape, 2) // 32 == iota(long.shape, 1), tail, 0.0)
    rows = dot_nn(weights[128:, :], values[:128, :]) + dot_nn(
        tail.reshape(64, 128).astype(BF16), values[128:, :]
    )
    for i in range(8):
        out[128 + 4 * i : 132 + 4 * i, :] = rows[8 * i : 8 * i + 4, :].astype(BF16)


def on_device(
    hidden, w_query, w_key, w_value, mix_before, mix_after, doc_lengths, doc_owner, loader_order
):
    depth = hidden.shape[1]
    grant = pltpu.CompilerParams(vmem_limit_bytes=12 << 20)
    packed = pltpu.CompilerParams(
        vmem_limit_bytes=12 << 20
    )
    rows = N_SEQ * PIECE
    vmem = pl.BlockSpec(memory_space=pltpu.VMEM)
    pair = np.arange(HEAD_DIM) // 2
    freq = jnp.asarray((THETA ** (-2.0 * pair / HEAD_DIM)).astype(np.float32)[None, :])
    lens = doc_lengths.reshape(1, TOK)
    own = doc_owner.reshape(1, TOK)
    order = loader_order.reshape(N_SEQ, TOK)

    hbm = pl.BlockSpec(memory_space=pltpu.HBM)
    table = jax.ShapeDtypeStruct((HEADS, HEADS, 128), F32)
    send, info, table_b, table_a = pl.pallas_call(
        project_kernel,
        in_specs=[hbm] * 10,
        out_specs=[vmem] * 4,
        out_shape=[
            jax.ShapeDtypeStruct((rows, HEAD_DIM), BF16),
            jax.ShapeDtypeStruct((8, TOK), F32),
            table,
            table,
        ],
        scratch_shapes=[
            pltpu.VMEM((TOK, depth), BF16),
            pltpu.VMEM((depth, HEAD_DIM), BF16),
            pltpu.VMEM((4 * KV_COLS, depth), BF16),
            pltpu.VMEM((1, TOK), jnp.int32),
            pltpu.VMEM((1, TOK), jnp.int32),
            pltpu.VMEM((N_SEQ, TOK), jnp.int32),
            pltpu.VMEM((1, TOK), F32),
            pltpu.VMEM((TOK, HEAD_DIM), F32),
            pltpu.VMEM((TOK, HEAD_DIM), F32),
            pltpu.VMEM((2, TOK, HEAD_DIM), F32),
            pltpu.VMEM((rows, 3 * TOK), BF16),
            pltpu.VMEM((HEADS, HEADS), F32),
            pltpu.VMEM((HEADS, HEADS), F32),
            pltpu.SemaphoreType.DMA((14,)),
        ],
        compiler_params=packed,
        name="project",
    )(
        *[
            pltpu.with_memory_space_constraint(x, pltpu.HBM)
            for x in (
                hidden, w_query, w_key.T, w_value.T, lens, own, order, freq, mix_before, mix_after,
            )
        ]
    )

    got = lax.all_to_all(
        send.reshape(N_SEQ, PIECE, HEAD_DIM), "seq", split_axis=0, concat_axis=0, tiled=True
    )
    gathered = lax.all_gather(got[:, PIECE - KV_ROWS :], "sub", axis=0, tiled=True)
    got = got.reshape(rows, HEAD_DIM)
    gathered = gathered.reshape(GROUP * N_SEQ * KV_ROWS, HEAD_DIM)

    logits, values = pl.pallas_call(
        functools.partial(logits_kernel, 1.0 / HEAD_DIM**0.5),
        in_specs=[vmem, vmem],
        out_specs=[vmem, vmem],
        out_shape=[
            jax.ShapeDtypeStruct((HEADS, 8, 128), F32),
            jax.ShapeDtypeStruct((rows, HEAD_DIM), BF16),
        ],
        compiler_params=packed,
        name="logits",
    )(got, gathered)

    mine = lax.all_to_all(logits, ("grp", "sub"), split_axis=0, concat_axis=0, tiled=True)
    blended = pl.pallas_call(
        soften_kernel,
        in_specs=[vmem] * 4,
        out_specs=vmem,
        out_shape=jax.ShapeDtypeStruct((HEADS, 8, 128), BF16),
        compiler_params=pltpu.CompilerParams(
            vmem_limit_bytes=12 << 20
        ),
        name="soften",
    )(mine, table_b, table_a, info)
    back = lax.all_to_all(blended, ("grp", "sub"), split_axis=0, concat_axis=0, tiled=True)
    return pl.pallas_call(
        output_kernel,
        in_specs=[vmem, vmem],
        out_specs=vmem,
        out_shape=jax.ShapeDtypeStruct((CAP, HEAD_DIM), BF16),
        compiler_params=grant,
        name="output",
    )(back.reshape(HEADS * 8, 128), values)


def solution(mesh):
    split = Mesh(mesh.devices.reshape(N_SEQ, HEADS // GROUP, GROUP), ("seq", "grp", "sub"))
    mp = ("grp", "sub")
    placed = (P("seq", None), P(None, mp), P(None, mp), P(None, mp), P(), P(), P(), P(), P())
    return jax.shard_map(
        on_device, mesh=split, in_specs=placed, out_specs=P("seq", mp), check_vma=False
    )
```
